32 devices in a mesh: dp: 4 (over x, core), fsdp: 8 (over z, y).
Axes of the slice: x: 2, y: 2, z: 4, core: 2. Of those that a mesh axis runs over, the one named last changes fastest.
Arguments:
- tokens: bfloat16 [16384, 768], P(('dp', 'fsdp')), may hold values from -6 to 6
- cotangent: bfloat16 [16384, 768], P(('dp', 'fsdp')), may hold values from -6 to 6
- tile_dest: int32 [128], P(('dp', 'fsdp')), may hold values from 0 to 31, as said below
- seq_lengths: int32 [32, 4], P(('dp', 'fsdp')), may hold values from 0 to 512, as said below
- norm1_gain: float32 [768], P(('dp', 'fsdp')), may hold values from 0.5 to 1.5
- norm1_bias: float32 [768], P(('dp', 'fsdp')), may hold values from -1.5 to 1.5
- w_qkv: float32 [768, 2304], P(('dp', 'fsdp')), may hold values from -0.3125 to 0.3125
- q_bias: float32 [768], P(('dp', 'fsdp')), may hold values from -1.5 to 1.5
- v_bias: float32 [768], P(('dp', 'fsdp')), may hold values from -1.5 to 1.5
- w_out: float32 [768, 768], P(('dp', 'fsdp')), may hold values from -0.75 to 0.75
- out_bias: float32 [768], P(('dp', 'fsdp')), may hold values from -1.5 to 1.5
- norm2_gain: float32 [768], P(('dp', 'fsdp')), may hold values from 0.5 to 1.5
- norm2_bias: float32 [768], P(('dp', 'fsdp')), may hold values from -1.5 to 1.5
- w_up: float32 [768, 3072], P(('dp', 'fsdp')), may hold values from -0.21875 to 0.21875
- up_bias: float32 [3072], P(('dp', 'fsdp')), may hold values from -1.5 to 1.5
- w_down: float32 [3072, 768], P(('dp', 'fsdp')), may hold values from -0.109375 to 0.109375
- down_bias: float32 [768], P(('dp', 'fsdp')), may hold values from -1.5 to 1.5
Outputs:
- mixed: bfloat16 [16384, 768], P(('dp', 'fsdp'))
- grad_tokens: bfloat16 [16384, 768], P(('dp', 'fsdp'))
- grad_norm1_gain: float32 [768], P(('dp', 'fsdp'))
- grad_norm1_bias: float32 [768], P(('dp', 'fsdp'))
- grad_w_qkv: float32 [768, 2304], P(('dp', 'fsdp'))
- grad_q_bias: float32 [768], P(('dp', 'fsdp'))
- grad_v_bias: float32 [768], P(('dp', 'fsdp'))
- grad_w_out: float32 [768, 768], P(('dp', 'fsdp'))
- grad_out_bias: float32 [768], P(('dp', 'fsdp'))
- grad_norm2_gain: float32 [768], P(('dp', 'fsdp'))
- grad_norm2_bias: float32 [768], P(('dp', 'fsdp'))
- grad_w_up: float32 [768, 3072], P(('dp', 'fsdp'))
- grad_up_bias: float32 [3072], P(('dp', 'fsdp'))
- grad_w_down: float32 [3072, 768], P(('dp', 'fsdp'))
- grad_down_bias: float32 [768], P(('dp', 'fsdp'))
The draws below stay inside these ranges and needn't reach their ends.
Inputs may be any that keep to these rules, and one draw needn't show every extreme that they name: `tile_dest`: within each dp index the entries of its 8 devices form a permutation of 0 to 31; entry e sends its tile to device e // 4 of that dp index, slot e % 4; the 4 tiles of one device go to 4 different devices, so each device sends at most one tile to each device and receives exactly 4. `seq_lengths`: on each device the tile counts ceil(length / 128) of the 4 slots sum to 4; empty slots occur; every dp index has a device holding one sequence of 512 tokens.
All inputs are finite; a program needn't handle non-finite values.
Results may differ from the reference program's by a relative error of at most 0.014.
The reference program's roundings to bfloat16 on the way count: a program that leaves them out, or rounds other values in their place, can miss the bound.
Values may be sent and summed in bfloat16 or wider, within the bound.
No kernel may reach another device: no remote copies, remote signals or barrier semaphores. Data moves between devices by JAX's collectives and lax.ppermute only.
A program may use at most 128 MiB of HBM per device.

```python
from functools import partial
import jax
import jax.numpy as jnp
from jax import lax

D = 768
HEADS = 12
HEAD_DIM = 64
FF = 3072
TILE = 128
TILES_DEV = 4
SEQ_DEV = 4
TOK_DEV = 512
PEERS = 8
GROUPS = 4
MESH_DEVS = 32
TOKENS = 16384


def draw_tile_dest(key, part):

    def one_group(group_key):
        sub_keys = jax.random.split(group_key, 4)
        outer_perm = jax.random.permutation(sub_keys[0], PEERS)
        inner_perm = jax.random.permutation(sub_keys[1], PEERS)
        offsets = jax.random.permutation(sub_keys[2], PEERS)[:TILES_DEV]
        perm_keys = jax.random.split(sub_keys[3], 2 * PEERS)
        slot_perm = jax.vmap(lambda one_key: jax.random.permutation(one_key, TILES_DEV))(perm_keys[:PEERS])
        order_perm = jax.vmap(lambda one_key: jax.random.permutation(one_key, TILES_DEV))(perm_keys[PEERS:])
        source = jnp.arange(PEERS)[:, None]
        target = outer_perm[(inner_perm[source] + offsets[order_perm]) % PEERS]
        slot_index = slot_perm[target, order_perm]
        return (target * TILES_DEV + slot_index).reshape(-1)
    group_keys = jax.random.split(key, GROUPS)
    return jax.vmap(one_group)(group_keys).reshape(-1).astype(jnp.int32)


def draw_seq_lengths(key, part):
    key_cuts, key_pick, key_pads = jax.random.split(key, 3)
    device_total = GROUPS * PEERS
    cuts = jnp.sort(jax.random.randint(key_cuts, (device_total, SEQ_DEV - 1), 0, TILES_DEV + 1), axis=1)
    bounds = jnp.concatenate([jnp.zeros((device_total, 1), jnp.int32), cuts.astype(jnp.int32), jnp.full((device_total, 1), TILES_DEV, jnp.int32)], axis=1)
    tile_counts = bounds[:, 1:] - bounds[:, :-1]
    chosen = jax.random.randint(key_pick, (GROUPS,), 0, PEERS) + jnp.arange(GROUPS) * PEERS
    full_row = jnp.any(jnp.arange(device_total)[:, None] == chosen[None, :], axis=1)
    first_slot = jnp.arange(SEQ_DEV)[None, :] == 0
    tile_counts = jnp.where(full_row[:, None], jnp.where(first_slot, TILES_DEV, 0), tile_counts)
    pads = jax.random.randint(key_pads, (device_total, SEQ_DEV), 0, TILE)
    pads = jnp.where(full_row[:, None], 0, pads)
    lengths = jnp.where(tile_counts > 0, tile_counts * TILE - pads, 0)
    return lengths.astype(jnp.int32)


def level_of(rng, shape, cuts, least, high):
    factor_of = 1.0
    for dim, shards_of in cuts:
        steps = jax.random.uniform(jax.random.fold_in(jax.random.fold_in(rng, 6), dim), (shards_of,), jnp.float32, least / len(cuts), high / len(cuts))
        factor_of = factor_of * jnp.repeat(jnp.exp(steps), shape[dim] // shards_of).reshape((-1,) + (1,) * (len(shape) - 1 - dim))
    return factor_of


def centred(stream_key, extent, deviation, reach, cuts=(), kind=jnp.bfloat16):
    loudness = level_of(stream_key, extent, cuts, -0.22, 0.18) if cuts else 1.0
    values = jax.random.normal(stream_key, extent, jnp.float32) * deviation * loudness
    return jnp.minimum(jnp.maximum(values, -reach), reach).astype(kind)


def setup_inputs(seed: int = 0) -> dict:
    streams_of = jax.random.split(jax.random.key(seed), 18)
    tokens = centred(streams_of[0], (TOKENS, D), 1.0, 6.0, ((0, 32),))
    cotangent = centred(streams_of[1], (TOKENS, D), 1.0, 6.0, ((0, 32),))
    tile_dest = draw_tile_dest(jax.random.fold_in(streams_of[17], 71), 0)
    seq_lengths = draw_seq_lengths(jax.random.fold_in(streams_of[17], 71), 0)
    norm1_gain = jnp.clip(1.0 + 0.1 * jax.random.normal(streams_of[4], (D,), jnp.float32), 0.5, 1.5)
    norm1_bias = centred(streams_of[5], (D,), 0.3, 1.5, ((0, 32),), jnp.float32)
    w_qkv = centred(streams_of[6], (D, 3 * D), (D // 2) ** -0.5, 0.3125, ((0, 32),), jnp.float32)
    q_bias = centred(streams_of[7], (D,), 0.3, 1.5, ((0, 32),), jnp.float32)
    v_bias = centred(streams_of[8], (D,), 0.3, 1.5, ((0, 32),), jnp.float32)
    w_out = centred(streams_of[9], (D, D), (D // 12) ** -0.5, 0.75, ((0, 32),), jnp.float32)
    out_bias = centred(streams_of[10], (D,), 0.3, 1.5, ((0, 32),), jnp.float32)
    norm2_gain = jnp.clip(1.0 + 0.1 * jax.random.normal(streams_of[11], (D,), jnp.float32), 0.5, 1.5)
    norm2_bias = centred(streams_of[12], (D,), 0.3, 1.5, ((0, 32),), jnp.float32)
    w_up = centred(streams_of[13], (D, FF), D ** -0.5, 0.21875, ((0, 32),), jnp.float32)
    up_bias = centred(streams_of[14], (FF,), 0.3, 1.5, ((0, 32),), jnp.float32)
    w_down = centred(streams_of[15], (FF, D), FF ** -0.5, 0.109375, ((0, 32),), jnp.float32)
    down_bias = centred(streams_of[16], (D,), 0.3, 1.5, ((0, 32),), jnp.float32)
    return {"tokens": tokens, "cotangent": cotangent, "tile_dest": tile_dest, "seq_lengths": seq_lengths, "norm1_gain": norm1_gain, "norm1_bias": norm1_bias, "w_qkv": w_qkv, "q_bias": q_bias, "v_bias": v_bias, "w_out": w_out, "out_bias": out_bias, "norm2_gain": norm2_gain, "norm2_bias": norm2_bias, "w_up": w_up, "up_bias": up_bias, "w_down": w_down, "down_bias": down_bias}


HIGH = lax.Precision.HIGHEST
SCALE = 0.125
EPSILON = 1e-06
MASKED = -1000000000.0

@jax.custom_vjp
def low(v):
    return lax.optimization_barrier(v.astype(jnp.bfloat16)).astype(jnp.float32)

@jax.custom_vjp
def low_back(v):
    return v

def low_keep(v):
    return (low(v), None)

def low_pass(kept, grad):
    return (grad,)

def back_keep(v):
    return (v, None)

def back_low(kept, grad):
    return (low(grad),)
low.defvjp(low_keep, low_pass)
low_back.defvjp(back_keep, back_low)

def normalize(stream, gain, shift):
    middle = lax.optimization_barrier(jnp.mean(stream, axis=-1, keepdims=True))
    centered = stream - middle
    spread = lax.optimization_barrier(jnp.mean(centered * centered, axis=-1, keepdims=True))
    return centered * lax.rsqrt(spread + EPSILON) * gain + shift

def layout(lengths, row_count, tile_rows):
    tile_counts = (lengths + tile_rows - 1) // tile_rows
    seg_ends = jnp.cumsum(tile_counts) * tile_rows
    seg_starts = seg_ends - tile_counts * tile_rows
    position = jnp.arange(row_count, dtype=jnp.int32)[:, None]
    inside = (position >= seg_starts[None, :]) & (position < seg_ends[None, :])
    segment = lax.optimization_barrier(jnp.sum((position >= seg_ends[None, :]).astype(jnp.int32), axis=1))
    offset = lax.optimization_barrier(jnp.sum(jnp.where(inside, position - seg_starts[None, :], 0), axis=1))
    length_here = lax.optimization_barrier(jnp.sum(jnp.where(inside, lengths[None, :], 0), axis=1))
    return (segment, offset < length_here)

def block(params, stream, segment, valid_rows):
    gain_one, shift_one, mat_qkv, bias_q, bias_v, mat_out, bias_out, gain_two, shift_two, mat_up, bias_up, mat_down, bias_down = params
    row_count, model_width = stream.shape
    norm_one = low(normalize(stream, gain_one, shift_one))
    qkv_shift = jnp.concatenate([bias_q, jnp.zeros_like(bias_q), bias_v])
    qkv_raw = jnp.dot(norm_one, mat_qkv, precision=HIGH) + qkv_shift
    qkv_low = low(low_back(qkv_raw))
    queries = qkv_low[:, :model_width].reshape(row_count, HEADS, HEAD_DIM)
    key_rows = qkv_low[:, model_width:2 * model_width].reshape(row_count, HEADS, HEAD_DIM)
    values = qkv_low[:, 2 * model_width:].reshape(row_count, HEADS, HEAD_DIM)
    scores = jnp.einsum('qhd,khd->hqk', queries, key_rows, precision=HIGH) * SCALE
    scores = low_back(scores)
    allowed_pairs = (segment[:, None] == segment[None, :]) & valid_rows[None, :]
    scores = jnp.where(allowed_pairs[None], scores, MASKED)
    row_top = lax.optimization_barrier(jnp.max(scores, axis=2, keepdims=True))
    exp_scores = jnp.exp(scores - row_top)
    attn_probs = low(exp_scores / lax.optimization_barrier(jnp.sum(exp_scores, axis=2, keepdims=True)))
    merged = jnp.einsum('hqk,khd->qhd', attn_probs, values, precision=HIGH).reshape(row_count, model_width)
    attn_out = low(low_back(merged))
    mid_stream = stream + low_back(jnp.dot(attn_out, mat_out, precision=HIGH) + bias_out)
    norm_two = low(normalize(mid_stream, gain_two, shift_two))
    pre_act = low_back(jnp.dot(norm_two, mat_up, precision=HIGH) + bias_up)
    act_low = low(jax.nn.gelu(pre_act, approximate=True))
    return mid_stream + low_back(jnp.dot(act_low, mat_down, precision=HIGH) + bias_down)

def reference(tokens, cotangent, tile_dest, seq_lengths, norm1_gain, norm1_bias, w_qkv, q_bias, v_bias, w_out, out_bias, norm2_gain, norm2_bias, w_up, up_bias, w_down, down_bias):
    tile_total = tile_dest.shape[0]
    model_width = tokens.shape[1]
    group_span = PEERS * TILES_DEV
    home_index = jnp.arange(tile_total, dtype=jnp.int32) // group_span * group_span + tile_dest.astype(jnp.int32)
    flat_tokens = tokens.astype(jnp.float32).reshape(tile_total, TILE, model_width)
    flat_cot = cotangent.astype(jnp.float32).reshape(tile_total, TILE, model_width)
    here_tokens = jnp.zeros_like(flat_tokens).at[home_index].set(flat_tokens).reshape(MESH_DEVS, TOK_DEV, model_width)
    here_cot = jnp.zeros_like(flat_cot).at[home_index].set(flat_cot).reshape(MESH_DEVS, TOK_DEV, model_width)
    segment, valid_rows = jax.vmap(lambda lengths: layout(lengths, TOK_DEV, TILE))(seq_lengths)
    params = (norm1_gain, norm1_bias, w_qkv, q_bias, v_bias, w_out, out_bias, norm2_gain, norm2_bias, w_up, up_bias, w_down, down_bias)
    params = tuple((weight.astype(jnp.float32) for weight in params))

    def forward(stream, weights):
        lowered = tuple((low(weight) for weight in weights))
        step_fn = jax.checkpoint(partial(block, lowered))

        def apply_block(packed):
            return step_fn(packed[0], packed[1], packed[2])
        return lax.map(apply_block, (stream, segment, valid_rows))
    result, pullback = jax.vjp(forward, here_tokens, params)
    grad_here, grad_params = pullback(here_cot * valid_rows[..., None].astype(jnp.float32))
    mixed = result.astype(jnp.bfloat16).reshape(tile_total, TILE, model_width)[home_index].reshape(tokens.shape)
    grad_tokens = grad_here.astype(jnp.bfloat16).reshape(tile_total, TILE, model_width)[home_index].reshape(tokens.shape)
    return (mixed, grad_tokens, grad_params[0], grad_params[1], grad_params[2], grad_params[3], grad_params[4], grad_params[5], grad_params[6], grad_params[7], grad_params[8], grad_params[9], grad_params[10], grad_params[11], grad_params[12])
```

```python
import functools

import jax
import jax.numpy as jnp
from jax import lax
from jax.experimental import pallas as pl
from jax.experimental.pallas import tpu as pltpu
from jax.sharding import PartitionSpec as P

HEAD_DIM = 64
LANES = 128
SCALE = 0.125
EPSILON = 1e-06
MASKED = -1000000000.0
F32 = jnp.float32
BF16 = jnp.bfloat16
AXES = ("dp", "fsdp")


def bits_of(size):
    return size.bit_length() - 1


class Cube:
    def __init__(self, dp_size, fs_size):
        self.size = {"dp": dp_size, "fsdp": fs_size}
        high_dp = [("dp", b) for b in range(1, bits_of(dp_size))]
        high_fs = [("fsdp", b) for b in range(1, bits_of(fs_size))]
        low_fs = [("fsdp", 0)]
        self.core = ("dp", 0)
        self.orders = (high_fs + high_dp + low_fs, high_fs + low_fs + high_dp)
        self.shared = len(high_fs)
        self.natural = [("dp", b) for b in reversed(range(bits_of(dp_size)))] + [
            ("fsdp", b) for b in reversed(range(bits_of(fs_size)))
        ]

    def swap(self, value, link):
        axis, bit = link
        pairs = [(i, i ^ (1 << bit)) for i in range(self.size[axis])]
        return lax.ppermute(value, axis, pairs)

    def my_bit(self, link):
        axis, bit = link
        return (lax.axis_index(axis) >> bit) & 1


def gather_parts(cube, shard, cut):
    held = shard[None]
    for link in cube.orders[0][: cube.shared]:
        held = jnp.concatenate([held, cube.swap(held, link)], axis=0)
    dim, at = cut
    parts = [
        lax.slice_in_dim(held, 0, at, axis=dim + 1),
        lax.slice_in_dim(held, at, shard.shape[dim], axis=dim + 1),
    ]
    for step in range(cube.shared, len(cube.orders[0])):
        moved = [cube.swap(parts[i], cube.orders[i][step]) for i in range(2)]
        parts = [jnp.concatenate([parts[i], moved[i]], axis=0) for i in range(2)]
    others = [cube.swap(part, cube.core) for part in parts]
    return [(parts[0], others[0]), (parts[1], others[1])]


def assemble(cube, halves, me, shapes, plan):
    dp_high = cube.size["dp"] // 2
    fs_size = cube.size["fsdp"]

    def slot(order, a, f):
        where = 0
        for k, (axis, bit) in enumerate(order):
            value = (a >> (bit - 1)) & 1 if axis == "dp" else (f >> bit) & 1
            where = where + (value << k)
        return where

    def kernel(me_ref, own_p, other_p, own_q, other_q, *out_refs):
        core = me_ref[0] & 1
        for out_ref, pieces in zip(out_refs, plan):
            for part, source, target in pieces:
                own, other = ((own_p, other_p), (own_q, other_q))[part]
                out_ref[(0, core, 0) + target] = own[(0,) + source]
                out_ref[(0, 1 - core, 0) + target] = other[(0,) + source]

    def spec(part):
        rows, width = halves[part][0].shape[1:]
        order = cube.orders[part]
        return pl.BlockSpec(
            (1, rows, width),
            lambda a, f, me_ref: (slot(order, a ^ (me_ref[0] >> 1), f ^ me_ref[1]), 0, 0),
        )

    outs = pl.pallas_call(
        kernel,
        out_shape=[
            jax.ShapeDtypeStruct((dp_high, 2, fs_size) + shape, BF16) for shape in shapes
        ],
        grid_spec=pltpu.PrefetchScalarGridSpec(
            num_scalar_prefetch=1,
            grid=(dp_high, fs_size),
            in_specs=[spec(0), spec(0), spec(1), spec(1)],
            out_specs=[
                pl.BlockSpec((1, 2, 1) + shape, lambda a, f, me_ref: (a, 0, f, 0, 0))
                for shape in shapes
            ],
        ),
        name="assemble",
    )(me, *halves[0], *halves[1])
    count = dp_high * 2 * fs_size
    return [out.reshape(count * shape[0], shape[1]) for out, shape in zip(outs, shapes)]


def scatter_sum(cube, parts, rows):
    state = []
    for i, part in enumerate(parts):
        bits = list(cube.natural)
        state.append((part.reshape((2,) * len(bits) + (rows[i], part.shape[1])), bits))
    links = [[cube.core] + list(reversed(order)) for order in cube.orders]
    for step in range(len(links[0])):
        last = step == len(links[0]) - 1
        new_state = []
        for i in range(2):
            value, bits = state[i]
            link = links[i][step]
            dim = bits.index(link)
            mine = cube.my_bit(link)
            give = lax.dynamic_index_in_dim(value, 1 - mine, dim, keepdims=False)
            keep = lax.dynamic_index_in_dim(value, mine, dim, keepdims=False)
            got = cube.swap(give, link)
            total = keep.astype(F32) + got.astype(F32)
            new_state.append(
                (total if last else total.astype(BF16), bits[:dim] + bits[dim + 1 :])
            )
        state = new_state
    return [value for value, _ in state]


def pick_tiles(arrays, index, count):
    def kernel(index_ref, *refs):
        half = len(refs) // 2
        for k in range(half):
            refs[half + k][...] = refs[k][...]

    shape = arrays[0].shape[1:]
    return pl.pallas_call(
        kernel,
        out_shape=[jax.ShapeDtypeStruct((count,) + shape, a.dtype) for a in arrays],
        grid_spec=pltpu.PrefetchScalarGridSpec(
            num_scalar_prefetch=1,
            grid=(count,),
            in_specs=[
                pl.BlockSpec((1,) + shape, lambda i, index_ref: (index_ref[i], 0, 0))
                for _ in arrays
            ],
            out_specs=[
                pl.BlockSpec((1,) + shape, lambda i, index_ref: (i, 0, 0)) for _ in arrays
            ],
        ),
        name="pick_tiles",
    )(index, *arrays)


def dot_nn(left, right):
    return jnp.dot(left, right, preferred_element_type=F32)


def dot_tn(left, right):
    return lax.dot_general(left, right, (((0,), (0,)), ((), ())), preferred_element_type=F32)


def dot_nt(left, right):
    return lax.dot_general(left, right, (((1,), (1,)), ((), ())), preferred_element_type=F32)


def attend_forward(qkv, query_segment, key_segment):
    rows, width = qkv.shape
    width = width // 3
    blocks = width // LANES

    def kernel(q_ref, k_ref, v_ref, qs_ref, ks_ref, out_ref, lse_ref):
        allowed = ks_ref[...] == qs_ref[...]
        q = q_ref[...] * SCALE
        k = k_ref[...]
        v_t = v_ref[...].T
        lane = lax.broadcasted_iota(jnp.int32, (1, LANES), 1)
        outs = []
        for h in range(LANES // HEAD_DIM):
            k_h = jnp.where(lane // HEAD_DIM == h, k, jnp.zeros_like(k))
            scores = jnp.where(allowed, dot_nt(k_h, q), MASKED)
            top = jnp.max(scores, axis=0, keepdims=True)
            weight = jnp.exp(scores - top)
            total = jnp.sum(weight, axis=0, keepdims=True)
            probs = (weight * (1.0 / total)).astype(BF16)
            outs.append(dot_nn(v_t[h * HEAD_DIM : (h + 1) * HEAD_DIM], probs))
            lse_ref[0, h : h + 1, :] = top + jnp.log(total)
        out_ref[...] = jnp.concatenate(outs, axis=0).T.astype(BF16)

    return pl.pallas_call(
        kernel,
        out_shape=[
            jax.ShapeDtypeStruct((rows, width), BF16),
            jax.ShapeDtypeStruct((blocks, LANES // HEAD_DIM, rows), F32),
        ],
        grid=(blocks,),
        in_specs=[
            pl.BlockSpec((rows, LANES), lambda i: (0, i)),
            pl.BlockSpec((rows, LANES), lambda i: (0, blocks + i)),
            pl.BlockSpec((rows, LANES), lambda i: (0, 2 * blocks + i)),
            pl.BlockSpec((1, rows), lambda i: (0, 0)),
            pl.BlockSpec((rows, 1), lambda i: (0, 0)),
        ],
        out_specs=[
            pl.BlockSpec((rows, LANES), lambda i: (0, i)),
            pl.BlockSpec((1, LANES // HEAD_DIM, rows), lambda i: (i, 0, 0)),
        ],
        name="attend_forward",
    )(qkv, qkv, qkv, query_segment, key_segment)


def attend_backward(qkv, d_attn, lse, query_segment, key_segment):
    rows, width = d_attn.shape
    blocks = width // LANES

    def kernel(q_ref, k_ref, v_ref, d_ref, lse_ref, qs_ref, ks_ref, dq_ref, dk_ref, dv_ref):
        allowed = ks_ref[...] == qs_ref[...]
        q = q_ref[...] * SCALE
        k = k_ref[...]
        v = v_ref[...]
        d_out = d_ref[...]
        k_t = k.T
        lane = lax.broadcasted_iota(jnp.int32, (1, LANES), 1)
        d_q, d_k, d_v = [], 0.0, 0.0
        for h in range(LANES // HEAD_DIM):
            here = lane // HEAD_DIM == h
            zero = jnp.zeros_like(k)
            k_h = jnp.where(here, k, zero)
            scores = dot_nt(k_h, q)
            probs = jnp.where(allowed, jnp.exp(scores - lse_ref[0, h : h + 1, :]), 0.0)
            d_out_h = jnp.where(here, d_out, zero)
            d_v = d_v + dot_nn(probs.astype(BF16), d_out_h)
            d_probs = dot_nt(v, d_out_h)
            inner = jnp.sum(probs * d_probs, axis=0, keepdims=True)
            d_scores = (probs * (d_probs - inner)).astype(BF16)
            d_k = d_k + dot_nn(d_scores, jnp.where(here, q, zero))
            d_q.append(dot_nn(k_t[h * HEAD_DIM : (h + 1) * HEAD_DIM], d_scores))
        dq_ref[...] = (jnp.concatenate(d_q, axis=0).T * SCALE).astype(BF16)
        dk_ref[...] = d_k.astype(BF16)
        dv_ref[...] = d_v.astype(BF16)

    head = pl.BlockSpec((rows, LANES), lambda i: (0, i))
    return pl.pallas_call(
        kernel,
        out_shape=[jax.ShapeDtypeStruct((rows, width), BF16)] * 3,
        grid=(blocks,),
        in_specs=[
            head,
            pl.BlockSpec((rows, LANES), lambda i: (0, blocks + i)),
            pl.BlockSpec((rows, LANES), lambda i: (0, 2 * blocks + i)),
            head,
            pl.BlockSpec((1, LANES // HEAD_DIM, rows), lambda i: (i, 0, 0)),
            pl.BlockSpec((1, rows), lambda i: (0, 0)),
            pl.BlockSpec((rows, 1), lambda i: (0, 0)),
        ],
        out_specs=[head] * 3,
        name="attend_backward",
    )(qkv, qkv, qkv, d_attn, lse, query_segment, key_segment)


def normalize(stream):
    middle = jnp.mean(stream, axis=-1, keepdims=True)
    centered = stream - middle
    spread = jnp.mean(centered * centered, axis=-1, keepdims=True)
    rho = lax.rsqrt(spread + EPSILON)
    return centered * rho, rho


def normalize_back(grad, gain, hat, rho):
    scaled = grad * gain
    return rho * (
        scaled
        - jnp.mean(scaled, axis=-1, keepdims=True)
        - hat * jnp.mean(scaled * hat, axis=-1, keepdims=True)
    )


def gelu_tanh(values):
    return jax.nn.gelu(values, approximate=True)


def layout(lengths, row_count, tile_rows):
    tile_counts = (lengths + tile_rows - 1) // tile_rows
    seg_ends = jnp.cumsum(tile_counts) * tile_rows
    seg_starts = seg_ends - tile_counts * tile_rows
    position = jnp.arange(row_count, dtype=jnp.int32)[:, None]
    inside = (position >= seg_starts[None, :]) & (position < seg_ends[None, :])
    segment = jnp.sum((position >= seg_ends[None, :]).astype(jnp.int32), axis=1)
    offset = jnp.sum(jnp.where(inside, position - seg_starts[None, :], 0), axis=1)
    length_here = jnp.sum(jnp.where(inside, lengths[None, :], 0), axis=1)
    return (segment, offset < length_here)


def col_sums(values):
    return jnp.sum(values.astype(F32), axis=0)


def per_device(
    tokens,
    cotangent,
    tile_dest,
    seq_lengths,
    norm1_gain,
    norm1_bias,
    w_qkv,
    q_bias,
    v_bias,
    w_out,
    out_bias,
    norm2_gain,
    norm2_bias,
    w_up,
    up_bias,
    w_down,
    down_bias,
):
    dp_size = lax.axis_size("dp")
    peer_count = lax.axis_size("fsdp")
    cube = Cube(dp_size, peer_count)
    my_dp, my_fs = lax.axis_index("dp"), lax.axis_index("fsdp")
    me = jnp.stack([my_dp, my_fs]).astype(jnp.int32)
    tile_count = tile_dest.shape[0]
    row_count, width = tokens.shape
    tile_rows = row_count // tile_count
    shard = w_qkv.shape[0]
    hidden = w_up.shape[1]
    hidden_shard = w_down.shape[0]
    spread = hidden // width

    small = [norm1_gain, norm1_bias, q_bias, v_bias, out_bias, norm2_gain, norm2_bias, down_bias]
    dest_column = jnp.zeros((shard,), F32).at[:tile_count].set(tile_dest.astype(F32))
    columns = jnp.concatenate(
        [jnp.stack(small + [dest_column], axis=1), up_bias.reshape(shard, spread)], axis=1
    )
    columns = jnp.pad(columns, ((0, 0), (0, LANES - columns.shape[1])))
    chunk_a = jnp.concatenate([w_qkv, w_out, columns], axis=1).astype(BF16)
    width_a = chunk_a.shape[1]
    cut_a = (width_a // 2 + LANES - 1) // LANES * LANES

    target = tile_dest // tile_count
    peer_ids = jnp.arange(peer_count, dtype=jnp.int32)
    sending = target[None, :] == peer_ids[:, None]
    give_index = jnp.sum(
        jnp.where(sending, jnp.arange(tile_count, dtype=jnp.int32)[None, :], 0), axis=1
    )
    tiled = (tile_count, tile_rows, width)
    bucket_tokens, bucket_cot = pick_tiles(
        [tokens.reshape(tiled), cotangent.reshape(tiled)], give_index, peer_count
    )

    def exchange(buckets):
        return lax.all_to_all(buckets, "fsdp", split_axis=0, concat_axis=0, tiled=True)

    got_tokens = exchange(bucket_tokens)
    full_a = gather_parts(cube, chunk_a, (1, cut_a))
    got_cot = exchange(bucket_cot)
    full_b = gather_parts(cube, w_up.astype(BF16), (1, hidden // 2))
    full_c = gather_parts(cube, w_down.astype(BF16), (0, hidden_shard // 2))

    def column_plan(start, stop):
        pieces = []
        every = slice(None)
        if start < cut_a:
            end = min(stop, cut_a)
            pieces.append((0, (every, slice(start, end)), (every, slice(0, end - start))))
        if stop > cut_a:
            begin = max(start, cut_a)
            pieces.append(
                (
                    1,
                    (every, slice(begin - cut_a, stop - cut_a)),
                    (every, slice(begin - start, stop - start)),
                )
            )
        return pieces

    wide = 3 * width
    mat_qkv, mat_out, vectors = assemble(
        cube,
        full_a,
        me,
        [(shard, wide), (shard, width), (shard, LANES)],
        [column_plan(0, wide), column_plan(wide, wide + width), column_plan(wide + width, width_a)],
    )
    every = slice(None)
    half = hidden // 2
    (mat_up,) = assemble(
        cube,
        full_b,
        me,
        [(shard, hidden)],
        [
            [
                (0, (every, slice(0, half)), (every, slice(0, half))),
                (1, (every, slice(0, half)), (every, slice(half, hidden))),
            ]
        ],
    )
    half_rows = hidden_shard // 2
    (mat_down,) = assemble(
        cube,
        full_c,
        me,
        [(hidden_shard, width)],
        [
            [
                (0, (every, every), (slice(0, half_rows), every)),
                (1, (every, every), (slice(half_rows, hidden_shard), every)),
            ]
        ],
    )
    vectors = vectors.astype(F32)
    gain_one, shift_one, bias_q, bias_v, bias_out, gain_two, shift_two, bias_down, dest_all = (
        vectors[:, :9].T
    )
    bias_up = vectors[:, 9 : 9 + spread].reshape(hidden)

    dest_all = dest_all.reshape(dp_size, peer_count, shard)[:, :, :tile_count].astype(jnp.int32)
    dest_here = lax.dynamic_index_in_dim(dest_all, my_dp, 0, keepdims=False)
    to_me = dest_here // tile_count == my_fs
    got_slot = jnp.sum(jnp.where(to_me, dest_here % tile_count + 1, 0), axis=1) - 1
    slots = jnp.arange(tile_count, dtype=jnp.int32)
    take_index = jnp.sum(
        jnp.where(got_slot[None, :] == slots[:, None], peer_ids[None, :], 0), axis=1
    )
    back_index = jnp.maximum(got_slot, 0)

    (local_tokens,) = pick_tiles([got_tokens], take_index, tile_count)
    (local_cot,) = pick_tiles([got_cot], take_index, tile_count)
    local_tokens = local_tokens.reshape(row_count, width)
    local_cot = local_cot.reshape(row_count, width)

    segment, valid_rows = layout(seq_lengths[0], row_count, tile_rows)
    query_segment = segment[None, :]
    key_segment = jnp.where(valid_rows, segment, -1)[:, None]

    stream = local_tokens.astype(F32)
    hat_one, rho_one = normalize(stream)
    norm_one = (hat_one * gain_one + shift_one).astype(BF16)
    qkv_shift = jnp.concatenate([bias_q, jnp.zeros((width,), F32), bias_v])
    qkv_low = (dot_nn(norm_one, mat_qkv) + qkv_shift).astype(BF16)
    attn_out, lse = attend_forward(qkv_low, query_segment, key_segment)
    mid_stream = stream + dot_nn(attn_out, mat_out) + bias_out
    hat_two, rho_two = normalize(mid_stream)
    norm_two = (hat_two * gain_two + shift_two).astype(BF16)
    pre_act = dot_nn(norm_two, mat_up) + bias_up
    act_value, gelu_pull = jax.vjp(gelu_tanh, pre_act)
    act_low = act_value.astype(BF16)
    result = (mid_stream + dot_nn(act_low, mat_down) + bias_down).astype(BF16)

    def send_back(rows_low):
        (buckets,) = pick_tiles([rows_low.reshape(tiled)], back_index, peer_count)
        return exchange(buckets)

    def receive_back(got):
        (tiles,) = pick_tiles([got], target, tile_count)
        return tiles.reshape(row_count, width)

    mixed = receive_back(send_back(result))

    grad_out_rows = local_cot.astype(F32) * valid_rows.astype(F32)[:, None]
    grad_out_low = grad_out_rows.astype(BF16)
    d_down_bias = col_sums(grad_out_low)
    d_w_down = dot_tn(act_low, grad_out_low).astype(BF16)
    d_act = dot_nt(grad_out_low, mat_down)
    d_pre = gelu_pull(d_act)[0].astype(BF16)
    d_up_bias = col_sums(d_pre)
    d_w_up = dot_tn(norm_two, d_pre).astype(BF16)
    d_norm_two = dot_nt(d_pre, mat_up)
    d_gain_two = jnp.sum(d_norm_two * hat_two, axis=0)
    d_shift_two = jnp.sum(d_norm_two, axis=0)
    d_mid = grad_out_rows + normalize_back(d_norm_two, gain_two, hat_two, rho_two)
    d_proj_low = d_mid.astype(BF16)
    d_out_bias = col_sums(d_proj_low)
    d_w_out = dot_tn(attn_out, d_proj_low).astype(BF16)
    d_attn = dot_nt(d_proj_low, mat_out).astype(BF16)

    devices = dp_size * peer_count
    d_w_down = d_w_down.reshape(devices, 2, half_rows, width)
    s_down = scatter_sum(
        cube,
        [d_w_down[:, i].reshape(devices * half_rows, width) for i in range(2)],
        [half_rows, half_rows],
    )
    s_up = scatter_sum(cube, [d_w_up[:, :half], d_w_up[:, half:]], [shard, shard])

    d_q, d_k, d_v = attend_backward(qkv_low, d_attn, lse, query_segment, key_segment)
    d_qkv = jnp.concatenate([d_q, d_k, d_v], axis=1)
    d_q_bias = col_sums(d_q)
    d_v_bias = col_sums(d_v)
    d_w_qkv = dot_tn(norm_one, d_qkv).astype(BF16)
    d_norm_one = dot_nt(d_qkv, mat_qkv)
    d_gain_one = jnp.sum(d_norm_one * hat_one, axis=0)
    d_shift_one = jnp.sum(d_norm_one, axis=0)
    d_stream = d_mid + normalize_back(d_norm_one, gain_one, hat_one, rho_one)
    grad_tokens = receive_back(send_back(d_stream.astype(BF16)))

    d_small = [
        d_gain_one,
        d_shift_one,
        d_q_bias,
        d_v_bias,
        d_out_bias,
        d_gain_two,
        d_shift_two,
        d_down_bias,
    ]
    d_columns = jnp.concatenate(
        [jnp.stack(d_small, axis=1), d_up_bias.reshape(width, spread)], axis=1
    )
    d_columns = jnp.pad(d_columns, ((0, 0), (0, LANES - d_columns.shape[1]))).astype(BF16)
    d_chunk_a = jnp.concatenate([d_w_qkv, d_w_out, d_columns], axis=1)
    s_a = scatter_sum(cube, [d_chunk_a[:, :cut_a], d_chunk_a[:, cut_a:]], [shard, shard])
    s_a = jnp.concatenate(s_a, axis=1)
    s_columns = s_a[:, wide + width :]
    s_small = s_columns[:, :8].T
    return (
        mixed,
        grad_tokens,
        s_small[0],
        s_small[1],
        s_a[:, :wide],
        s_small[2],
        s_small[3],
        s_a[:, wide : wide + width],
        s_small[4],
        s_small[5],
        s_small[6],
        jnp.concatenate(s_up, axis=1),
        s_columns[:, 8 : 8 + spread].reshape(hidden_shard),
        jnp.concatenate(s_down, axis=0),
        s_small[7],
    )


def solution(mesh):
    rows, matrix = P(AXES), P(AXES, None)
    in_specs = (
        matrix,
        matrix,
        rows,
        matrix,
        rows,
        rows,
        matrix,
        rows,
        rows,
        matrix,
        rows,
        rows,
        rows,
        matrix,
        rows,
        matrix,
        rows,
    )
    out_specs = (
        matrix,
        matrix,
        rows,
        rows,
        matrix,
        rows,
        rows,
        matrix,
        rows,
        rows,
        rows,
        matrix,
        rows,
        matrix,
        rows,
    )
    return jax.shard_map(
        per_device, mesh=mesh, in_specs=in_specs, out_specs=out_specs, check_vma=False
    )
```

```python
import functools

import jax
import jax.numpy as jnp
from jax import lax
from jax.experimental import pallas as pl
from jax.experimental.pallas import tpu as pltpu
from jax.sharding import PartitionSpec as P

HEAD_DIM = 64
LANES = 128
SCALE = 0.125
EPSILON = 1e-06
MASKED = -1000000000.0
F32 = jnp.float32
BF16 = jnp.bfloat16
AXES = ("dp", "fsdp")


def bits_of(size):
    return size.bit_length() - 1


class Cube:
    def __init__(self, dp_size, fs_size):
        self.size = {"dp": dp_size, "fsdp": fs_size}
        self.dp_high, self.fs_size = dp_size // 2, fs_size
        high_dp = [("dp", b) for b in reversed(range(1, bits_of(dp_size)))]
        low_fs = [("fsdp", 0)]
        self.core = ("dp", 0)
        self.far = [("fsdp", b) for b in reversed(range(1, bits_of(fs_size)))]
        self.near = (high_dp + low_fs, low_fs + high_dp)
        self.natural = high_dp + self.far + low_fs

    def swap(self, value, link):
        axis, bit = link
        pairs = [(i, i ^ (1 << bit)) for i in range(self.size[axis])]
        return lax.ppermute(value, axis, pairs)

    def masks(self, slot, order):
        found = {"dp": 0, "fsdp": 0}
        for k, (axis, bit) in enumerate(order):
            found[axis] |= ((slot >> k) & 1) << bit
        return found["dp"] >> 1, found["fsdp"]


def move(name, scalars, sources, out_shapes, plan):
    count = len(sources)
    total = sum(2 * s.size * s.dtype.itemsize for s in out_shapes)

    def kernel(scalar_ref, *refs):
        srcs, outs = refs[:count], refs[count : count + len(out_shapes)]
        sems = refs[-1]
        copies = [
            pltpu.make_async_copy(src, out, sems.at[i])
            for i, (src, out) in enumerate(plan(scalar_ref, srcs, outs))
        ]
        for copy in copies:
            copy.start()
        for copy in copies:
            copy.wait()

    class Counter:
        def __getitem__(self, key):
            return jnp.int32(0)

    class Blank:
        @property
        def at(self):
            return self

        def __getitem__(self, key):
            return self

    copies = len(
        plan(Counter(), [Blank() for _ in sources], [Blank() for _ in out_shapes])
    )
    return pl.pallas_call(
        kernel,
        out_shape=out_shapes,
        in_specs=[pl.BlockSpec(memory_space=pltpu.SMEM)]
        + [pl.BlockSpec(memory_space=pl.ANY) for _ in sources],
        out_specs=[pl.BlockSpec(memory_space=pltpu.VMEM) for _ in out_shapes],
        scratch_shapes=[pltpu.SemaphoreType.DMA((copies,))],
        cost_estimate=pl.CostEstimate(flops=0, transcendentals=0, bytes_accessed=total),
        name=name,
    )(scalars, *sources)


def after(value, *others):
    return lax.optimization_barrier((value,) + others)[0]


def tied(values, *others):
    if not others:
        return list(values)
    return list(lax.optimization_barrier(tuple(values) + others)[: len(values)])


class Gather:
    def __init__(self, cube, shard, cut):
        self.cube, self.bounds = cube, (0, cut, shard.shape[1])
        self.parts, self.moved = [shard[None]], []
        self.steps = [[link] for link in cube.far] + [list(pair) for pair in zip(*cube.near)]
        self.step = 0

    def advance(self, *others):
        links, count = self.steps[self.step], len(self.parts)
        parts = tied(self.parts + self.moved, *others)
        parts, moved = parts[:count], parts[count:]
        if moved:
            parts = [jnp.concatenate(pair, axis=0) for pair in zip(parts, moved)]
        if len(links) > len(parts):
            bounds = self.bounds
            parts = [lax.slice_in_dim(parts[0], bounds[i], bounds[i + 1], axis=2) for i in range(2)]
        self.parts = parts
        self.moved = [self.cube.swap(part, link) for part, link in zip(parts, links)]
        self.step += 1
        return self.moved

    def cores(self, *others):
        parts = tied(self.parts + self.moved, *others)
        self.parts = [parts[0], parts[2], parts[1], parts[3]]
        self.others = [self.cube.swap(part, self.cube.core) for part in self.parts]
        return self.others

    def matrices(self, me, pieces, *others):
        cube, bounds = self.cube, self.bounds
        half, rows = self.parts[0].shape[:2]

        def plan(me_ref, srcs, outs):
            core = me_ref[0] & 1
            pairs = []
            for i in range(2):
                order = cube.far + cube.near[i]
                for out, (first, wide, blocks) in zip(outs, pieces):
                    each = wide // blocks
                    for j in range(blocks):
                        low = max(bounds[i], first + j * each)
                        high = min(bounds[i + 1], first + (j + 1) * each)
                        if low >= high:
                            continue
                        taken = pl.ds(low - bounds[i], high - low)
                        placed = pl.ds(low - first - j * each, high - low)
                        for slot in range(2 * half):
                            mask_a, mask_f = cube.masks(slot, order)
                            a, f = (me_ref[0] >> 1) ^ mask_a, me_ref[1] ^ mask_f
                            for k in range(2):
                                src = srcs[4 * k + 2 * i + slot // half].at[slot % half, :, taken]
                                pairs.append((src, out.at[a, core ^ k, f, j, :, placed]))
            return pairs

        shapes = [
            jax.ShapeDtypeStruct(
                (cube.dp_high, 2, cube.fs_size, blocks, rows, wide // blocks), BF16
            )
            for _, wide, blocks in pieces
        ]
        sources = tied(self.parts + self.others, *others)
        outs = move("interleave", me, sources, shapes, plan)
        return [out.reshape(-1, out.shape[-1]) for out in outs]


def deal_apart(name, scalars, tiles, peer_count):
    count, shape = tiles.shape[0], tiles.shape[1:]

    def kernel(far_ref, src, *refs):
        outs, held, sems = refs[:peer_count], refs[-2], refs[-1]
        into = [pltpu.make_async_copy(src.at[i], held.at[i], sems.at[0, i]) for i in range(count)]
        for copy in into:
            copy.start()
        for i in range(count):
            into[i].wait()
            for d in range(peer_count):

                @pl.when(far_ref[i] == d)
                def _():
                    pltpu.make_async_copy(held.at[i], outs[d], sems.at[1, i]).start()

        for i in range(count):
            pltpu.make_async_copy(held.at[i], outs[0], sems.at[1, i]).wait()

    return pl.pallas_call(
        kernel,
        out_shape=[jax.ShapeDtypeStruct(shape, tiles.dtype)] * peer_count,
        in_specs=[pl.BlockSpec(memory_space=pltpu.SMEM), pl.BlockSpec(memory_space=pl.ANY)],
        out_specs=[pl.BlockSpec(memory_space=pl.ANY)] * peer_count,
        scratch_shapes=[
            pltpu.VMEM((count,) + shape, tiles.dtype),
            pltpu.SemaphoreType.DMA((2, count)),
        ],
        cost_estimate=pl.CostEstimate(
            flops=0, transcendentals=0, bytes_accessed=4 * tiles.size
        ),
        name=name,
    )(scalars, tiles)


def collect(name, scalars, buckets, count):
    shape, dtype = buckets[0].shape, buckets[0].dtype
    peer_count = len(buckets)

    def kernel(far_ref, *refs):
        srcs, out, held, sems = refs[:peer_count], refs[peer_count], refs[-2], refs[-1]
        back = [pltpu.make_async_copy(held.at[i], out.at[i], sems.at[1, i]) for i in range(count)]
        for i in range(count):
            for d in range(peer_count):

                @pl.when(far_ref[i] == d)
                def _():
                    pltpu.make_async_copy(srcs[d], held.at[i], sems.at[0, i]).start()

        for i in range(count):
            pltpu.make_async_copy(srcs[0], held.at[i], sems.at[0, i]).wait()
            back[i].start()
        for copy in back:
            copy.wait()

    return pl.pallas_call(
        kernel,
        out_shape=jax.ShapeDtypeStruct((count,) + shape, dtype),
        in_specs=[pl.BlockSpec(memory_space=pltpu.SMEM)]
        + [pl.BlockSpec(memory_space=pl.ANY)] * peer_count,
        out_specs=pl.BlockSpec(memory_space=pl.ANY),
        scratch_shapes=[
            pltpu.VMEM((count,) + shape, dtype),
            pltpu.SemaphoreType.DMA((2, count)),
        ],
        cost_estimate=pl.CostEstimate(
            flops=0, transcendentals=0, bytes_accessed=4 * count * buckets[0].size
        ),
        name=name,
    )(scalars, *buckets)


def deal_apart(name, scalars, tiles, peer_count):
    count, shape = tiles.shape[0], tiles.shape[1:]

    def kernel(far_ref, src, *refs):
        outs, held, sems = refs[:peer_count], refs[-2], refs[-1]
        into = [pltpu.make_async_copy(src.at[i], held.at[i], sems.at[0, i]) for i in range(count)]
        for copy in into:
            copy.start()
        for i in range(count):
            into[i].wait()
            for d in range(peer_count):

                @pl.when(far_ref[i] == d)
                def _():
                    pltpu.make_async_copy(held.at[i], outs[d], sems.at[1, i]).start()

        for i in range(count):
            pltpu.make_async_copy(held.at[i], outs[0], sems.at[1, i]).wait()

    return pl.pallas_call(
        kernel,
        out_shape=[jax.ShapeDtypeStruct(shape, tiles.dtype)] * peer_count,
        in_specs=[pl.BlockSpec(memory_space=pltpu.SMEM), pl.BlockSpec(memory_space=pl.ANY)],
        out_specs=[pl.BlockSpec(memory_space=pl.ANY)] * peer_count,
        scratch_shapes=[
            pltpu.VMEM((count,) + shape, tiles.dtype),
            pltpu.SemaphoreType.DMA((2, count)),
        ],
        cost_estimate=pl.CostEstimate(
            flops=0, transcendentals=0, bytes_accessed=4 * tiles.size
        ),
        name=name,
    )(scalars, tiles)


def collect(name, scalars, buckets, count):
    shape, dtype = buckets[0].shape, buckets[0].dtype
    peer_count = len(buckets)

    def kernel(far_ref, *refs):
        srcs, out, held, sems = refs[:peer_count], refs[peer_count], refs[-2], refs[-1]
        back = [pltpu.make_async_copy(held.at[i], out.at[i], sems.at[1, i]) for i in range(count)]
        for i in range(count):
            for d in range(peer_count):

                @pl.when(far_ref[i] == d)
                def _():
                    pltpu.make_async_copy(srcs[d], held.at[i], sems.at[0, i]).start()

        for i in range(count):
            pltpu.make_async_copy(srcs[0], held.at[i], sems.at[0, i]).wait()
            back[i].start()
        for copy in back:
            copy.wait()

    return pl.pallas_call(
        kernel,
        out_shape=jax.ShapeDtypeStruct((count,) + shape, dtype),
        in_specs=[pl.BlockSpec(memory_space=pltpu.SMEM)]
        + [pl.BlockSpec(memory_space=pl.ANY)] * peer_count,
        out_specs=pl.BlockSpec(memory_space=pl.ANY),
        scratch_shapes=[
            pltpu.VMEM((count,) + shape, dtype),
            pltpu.SemaphoreType.DMA((2, count)),
        ],
        cost_estimate=pl.CostEstimate(
            flops=0, transcendentals=0, bytes_accessed=4 * count * buckets[0].size
        ),
        name=name,
    )(scalars, *buckets)


def deal(name, peers, tiles, buckets):
    source = buckets if tiles is None else tiles
    count, shape = peers.shape[0], source.shape[1:]
    out_count = count if tiles is None else buckets

    def kernel(peers_ref, src, out, held, sems):
        into, back = [], []
        for i in range(count):
            peer = peers_ref[i]
            here, there = (peer, i) if tiles is None else (i, peer)
            into.append(pltpu.make_async_copy(src.at[here], held.at[i], sems.at[0, i]))
            back.append(pltpu.make_async_copy(held.at[i], out.at[there], sems.at[1, i]))
        for copy in into:
            copy.start()
        for first, second in zip(into, back):
            first.wait()
            second.start()
        for copy in back:
            copy.wait()

    return pl.pallas_call(
        kernel,
        out_shape=jax.ShapeDtypeStruct((out_count,) + shape, source.dtype),
        in_specs=[pl.BlockSpec(memory_space=pltpu.SMEM), pl.BlockSpec(memory_space=pl.ANY)],
        out_specs=pl.BlockSpec(memory_space=pl.ANY),
        scratch_shapes=[
            pltpu.VMEM((count,) + shape, source.dtype),
            pltpu.SemaphoreType.DMA((2, count)),
        ],
        cost_estimate=pl.CostEstimate(
            flops=0, transcendentals=0, bytes_accessed=4 * source.size // source.shape[0] * count
        ),
        name=name,
    )(peers, source)


def scatter_split(cube, me, grads, rows):
    slots = cube.dp_high * cube.fs_size
    order = cube.natural[::-1]
    views = [
        g.reshape(cube.dp_high, 2, cube.fs_size, blocks, rows, g.shape[1]) for g, blocks in grads
    ]
    width = sum(v.shape[3] * v.shape[5] for v in views)

    def split(me_ref, srcs, outs):
        core = me_ref[0] & 1
        pairs = []
        for k, out in enumerate(outs):
            for slot in range(slots):
                mask_a, mask_f = cube.masks(slot, order)
                a, f = (me_ref[0] >> 1) ^ mask_a, me_ref[1] ^ mask_f
                first = 0
                for src, view in zip(srcs, views):
                    for j in range(view.shape[3]):
                        columns = pl.ds(first, view.shape[5])
                        pairs.append((src.at[a, core ^ (1 - k), f, j], out.at[slot, :, columns]))
                        first += view.shape[5]
        return pairs

    shape = jax.ShapeDtypeStruct((slots, rows, width), BF16)
    return move("split", me, views, [shape, shape], split)


class Scatter:
    def __init__(self, cube, give, keep, cut):
        self.cube, self.cut = cube, cut
        self.give, self.keep = [give], [keep]
        self.left = [cube.natural[::-1]]
        self.plan = [[cube.core]] + [list(pair) for pair in zip(cube.near[0][::-1], cube.near[1][::-1])]
        self.plan += [[link] for link in cube.far[::-1]]
        self.step = 0

    def start(self):
        links = self.plan[self.step]
        return [self.cube.swap(give, link) for give, link in zip(self.give, links)]

    def finish(self, got, pieces=None):
        self.step += 1
        rows = self.keep[0].shape[1]
        widths = [k.shape[2] for k in self.keep]
        copies = []
        if self.step == len(self.plan):
            shapes = [
                jax.ShapeDtypeStruct((blocks * rows, wide // blocks), F32)
                for _, wide, blocks in pieces
            ]
            for o, (first, wide, blocks) in enumerate(pieces):
                each = wide // blocks
                for j in range(blocks):
                    low = first + j * each
                    target = (slice(j * rows, (j + 1) * rows), slice(None))
                    copies.append((0, 0, slice(low, low + each), o, target))
            return self.add(got, shapes, copies)
        links = self.plan[self.step]
        if len(links) > len(widths):
            ranges = [(0, 0, self.cut, 0, 0), (0, self.cut, widths[0], 1, 0)]
            self.left = [self.left[0], list(self.left[0])]
            new_widths = [self.cut, widths[0] - self.cut]
        elif len(links) < len(widths):
            ranges = [(0, 0, widths[0], 0, 0), (1, 0, widths[1], 0, widths[0])]
            new_widths = [sum(widths)]
        else:
            ranges = [(i, 0, w, i, 0) for i, w in enumerate(widths)]
            new_widths = widths
        slots = self.keep[0].shape[0]
        for source, low, high, part, first in ranges:
            bit = self.left[part].index(links[part])
            for slot in range(slots):
                side, rest = (slot >> bit) & 1, (slot >> (bit + 1) << bit) | (slot & ((1 << bit) - 1))
                target = (rest, slice(None), slice(first, first + high - low))
                copies.append((source, slot, slice(low, high), 2 * part + side, target))
        shapes = [
            jax.ShapeDtypeStruct((slots // 2, rows, w), BF16) for w in new_widths for _ in range(2)
        ]
        outs = self.add(got, shapes, copies)
        self.keep, self.give = outs[0::2], outs[1::2]
        self.left = [
            [link for link in self.left[i] if link != links[i]] for i in range(len(links))
        ]
        return None

    def add(self, got, shapes, copies):
        count = len(got)
        if self.keep[0].shape[0] <= 2:
            rows = {}
            for source, slot, columns, o, target in copies:
                mine = self.keep[source][slot, :, columns].astype(F32)
                total = (mine + got[source][slot, :, columns].astype(F32)).astype(shapes[o].dtype)
                rows.setdefault(o, []).append(total)
            outs = []
            for o, shape in enumerate(shapes):
                value = rows[o][0] if len(rows[o]) == 1 else jnp.concatenate(rows[o], axis=0)
                outs.append(value.reshape(shape.shape))
            return outs

        def kernel(*refs):
            outs = refs[2 * count :]
            for source, slot, columns, o, target in copies:
                mine = refs[source][slot, :, columns].astype(F32)
                came = refs[count + source][slot, :, columns].astype(F32)
                outs[o][target] = (mine + came).astype(outs[o].dtype)

        total = sum(2 * v.size * 2 for v in self.keep)
        return pl.pallas_call(
            kernel,
            out_shape=shapes,
            in_specs=[pl.BlockSpec(memory_space=pltpu.VMEM)] * (2 * count),
            out_specs=[pl.BlockSpec(memory_space=pltpu.VMEM)] * len(shapes),
            cost_estimate=pl.CostEstimate(
                flops=total // 4, transcendentals=0, bytes_accessed=3 * total // 2
            ),
            name="add_step",
        )(*self.keep, *got)


def dot_nn(left, right):
    return jnp.dot(left, right, preferred_element_type=F32)


def dot_tn(left, right):
    return lax.dot_general(left, right, (((0,), (0,)), ((), ())), preferred_element_type=F32)


def dot_nt(left, right):
    return lax.dot_general(left, right, (((1,), (1,)), ((), ())), preferred_element_type=F32)


def attend_forward(qkv, query_segment, key_segment):
    rows, width = qkv.shape
    width = width // 3
    blocks = width // LANES

    def kernel(q_ref, k_ref, v_ref, qs_ref, ks_ref, out_ref, lse_ref):
        allowed = ks_ref[...] == qs_ref[...]
        q = q_ref[...] * SCALE
        k = k_ref[...]
        v_t = v_ref[...].T
        lane = lax.broadcasted_iota(jnp.int32, (1, LANES), 1)
        outs = []
        for h in range(LANES // HEAD_DIM):
            k_h = jnp.where(lane // HEAD_DIM == h, k, jnp.zeros_like(k))
            scores = jnp.where(allowed, dot_nt(k_h, q), MASKED)
            top = jnp.max(scores, axis=0, keepdims=True)
            weight = jnp.exp(scores - top)
            total = jnp.sum(weight, axis=0, keepdims=True)
            probs = (weight * (1.0 / total)).astype(BF16)
            outs.append(dot_nn(v_t[h * HEAD_DIM : (h + 1) * HEAD_DIM], probs))
            lse_ref[0, h : h + 1, :] = top + jnp.log(total)
        out_ref[...] = jnp.concatenate(outs, axis=0).T.astype(BF16)

    return pl.pallas_call(
        kernel,
        out_shape=[
            jax.ShapeDtypeStruct((rows, width), BF16),
            jax.ShapeDtypeStruct((blocks, LANES // HEAD_DIM, rows), F32),
        ],
        grid=(blocks,),
        in_specs=[
            pl.BlockSpec((rows, LANES), lambda i: (0, i)),
            pl.BlockSpec((rows, LANES), lambda i: (0, blocks + i)),
            pl.BlockSpec((rows, LANES), lambda i: (0, 2 * blocks + i)),
            pl.BlockSpec((1, rows), lambda i: (0, 0)),
            pl.BlockSpec((rows, 1), lambda i: (0, 0)),
        ],
        out_specs=[
            pl.BlockSpec((rows, LANES), lambda i: (0, i)),
            pl.BlockSpec((1, LANES // HEAD_DIM, rows), lambda i: (i, 0, 0)),
        ],
        name="attend_forward",
    )(qkv, qkv, qkv, query_segment, key_segment)


def attend_backward(qkv, d_attn, lse, query_segment, key_segment):
    rows, width = d_attn.shape
    blocks = width // LANES

    def kernel(q_ref, k_ref, v_ref, d_ref, lse_ref, qs_ref, ks_ref, out_ref):
        allowed = ks_ref[...] == qs_ref[...]
        q = q_ref[...] * SCALE
        k = k_ref[...]
        v = v_ref[...]
        d_out = d_ref[...]
        k_t = k.T
        lane = lax.broadcasted_iota(jnp.int32, (1, LANES), 1)
        d_q, d_k, d_v = [], 0.0, 0.0
        for h in range(LANES // HEAD_DIM):
            here = lane // HEAD_DIM == h
            zero = jnp.zeros_like(k)
            k_h = jnp.where(here, k, zero)
            scores = dot_nt(k_h, q)
            probs = jnp.where(allowed, jnp.exp(scores - lse_ref[0, h : h + 1, :]), 0.0)
            d_out_h = jnp.where(here, d_out, zero)
            d_v = d_v + dot_nn(probs.astype(BF16), d_out_h)
            d_probs = dot_nt(v, d_out_h)
            inner = jnp.sum(probs * d_probs, axis=0, keepdims=True)
            d_scores = (probs * (d_probs - inner)).astype(BF16)
            d_k = d_k + dot_nn(d_scores, jnp.where(here, q, zero))
            d_q.append(dot_nn(k_t[h * HEAD_DIM : (h + 1) * HEAD_DIM], d_scores))
        d_q = jnp.concatenate(d_q, axis=0).T * SCALE
        for part, value in enumerate((d_q, d_k, d_v)):
            place = pl.multiple_of((pl.program_id(0) + part * blocks) * LANES, LANES)
            out_ref[:, pl.ds(place, LANES)] = value.astype(BF16)

    return pl.pallas_call(
        kernel,
        out_shape=jax.ShapeDtypeStruct((rows, 3 * width), BF16),
        grid=(blocks,),
        in_specs=[
            pl.BlockSpec((rows, LANES), lambda i: (0, i)),
            pl.BlockSpec((rows, LANES), lambda i: (0, blocks + i)),
            pl.BlockSpec((rows, LANES), lambda i: (0, 2 * blocks + i)),
            pl.BlockSpec((rows, LANES), lambda i: (0, i)),
            pl.BlockSpec((1, LANES // HEAD_DIM, rows), lambda i: (i, 0, 0)),
            pl.BlockSpec((1, rows), lambda i: (0, 0)),
            pl.BlockSpec((rows, 1), lambda i: (0, 0)),
        ],
        out_specs=pl.BlockSpec((rows, 3 * width), lambda i: (0, 0)),
        name="attend_backward",
    )(qkv, qkv, qkv, d_attn, lse, query_segment, key_segment)


def normalize(stream):
    middle = jnp.mean(stream, axis=-1, keepdims=True)
    centered = stream - middle
    spread = jnp.mean(centered * centered, axis=-1, keepdims=True)
    rho = lax.rsqrt(spread + EPSILON)
    return centered * rho, rho


def normalize_back(grad, gain, hat, rho):
    scaled = grad * gain
    return rho * (
        scaled
        - jnp.mean(scaled, axis=-1, keepdims=True)
        - hat * jnp.mean(scaled * hat, axis=-1, keepdims=True)
    )


def gelu_tanh(values):
    return jax.nn.gelu(values, approximate=True)


def layout(lengths, row_count, tile_rows):
    tile_counts = (lengths + tile_rows - 1) // tile_rows
    seg_ends = jnp.cumsum(tile_counts) * tile_rows
    seg_starts = seg_ends - tile_counts * tile_rows
    position = jnp.arange(row_count, dtype=jnp.int32)[:, None]
    inside = (position >= seg_starts[None, :]) & (position < seg_ends[None, :])
    segment = jnp.sum((position >= seg_ends[None, :]).astype(jnp.int32), axis=1)
    offset = jnp.sum(jnp.where(inside, position - seg_starts[None, :], 0), axis=1)
    length_here = jnp.sum(jnp.where(inside, lengths[None, :], 0), axis=1)
    return (segment, offset < length_here)


def col_sums(values):
    return jnp.sum(values.astype(F32), axis=0, keepdims=True)


def per_device(
    tokens,
    cotangent,
    tile_dest,
    seq_lengths,
    norm1_gain,
    norm1_bias,
    w_qkv,
    q_bias,
    v_bias,
    w_out,
    out_bias,
    norm2_gain,
    norm2_bias,
    w_up,
    up_bias,
    w_down,
    down_bias,
):
    dp_size = lax.axis_size("dp")
    peer_count = lax.axis_size("fsdp")
    cube = Cube(dp_size, peer_count)
    my_dp, my_fs = lax.axis_index("dp"), lax.axis_index("fsdp")
    me = jnp.stack([my_dp, my_fs]).astype(jnp.int32)
    tile_count = tile_dest.shape[0]
    row_count, width = tokens.shape
    tile_rows = row_count // tile_count
    shard = w_qkv.shape[0]
    hidden = w_up.shape[1]
    hidden_shard = w_down.shape[0]
    spread = hidden // width

    small = [norm1_gain, norm1_bias, q_bias, v_bias, out_bias, norm2_gain, norm2_bias, down_bias]
    dest_row = jnp.pad(tile_dest.astype(F32), (0, shard - tile_count))
    block = jnp.concatenate(
        [v.reshape(1, shard) for v in small + [dest_row]] + [up_bias.reshape(spread, shard)], axis=0
    )
    block_rows = block.shape[0]
    groups = -(-block_rows // shard)
    block = jnp.pad(block, ((0, groups * shard - block_rows), (0, LANES - shard)))
    if groups > 1:
        block = jnp.concatenate(jnp.split(block, groups, axis=0), axis=1)
    block_width = groups * LANES
    target = tile_dest // tile_count
    tiled = (tile_count, tile_rows, width)
    bucketed = (peer_count, tile_rows, width)

    wide = 3 * width
    half = hidden // 2
    chunk_a = jnp.concatenate([w_qkv, block], axis=1).astype(BF16)
    pieces = [w_out] + [w_up[:, j * width : (j + 1) * width] for j in range(spread)] + [w_down]
    chunk_b = jnp.concatenate([p.astype(BF16) for p in pieces], axis=0)
    full = lax.all_gather(chunk_b, AXES, axis=0, tiled=False)
    mat_out = full[:, :shard].reshape(-1, width)
    mat_up = jnp.concatenate(
        [full[:, (1 + j) * shard : (2 + j) * shard].reshape(-1, width) for j in range(spread)], axis=1
    )
    mat_down = full[:, (1 + spread) * shard :].reshape(hidden, width)
    distance = target ^ my_fs
    token_tiles = after(tokens.reshape(tiled), chunk_a)
    buckets = deal_apart("deal_tokens", distance, token_tiles, peer_count)

    def cross(bucket, d):
        return lax.ppermute(bucket, "fsdp", [(i, i ^ d) for i in range(peer_count)])

    cut_a = (chunk_a.shape[1] // 2 + LANES - 1) // LANES * LANES
    ga = Gather(cube, chunk_a, cut_a)
    steps = len(ga.steps)
    far = sorted(range(peer_count // 2, peer_count), key=lambda d: (d & 1, d))
    near = list(range(1, peer_count // 2))
    groups = [far[k::steps] + near[k::steps] for k in range(steps)]
    got = {0: buckets[0]}
    came_a, landed = [], []
    for k in range(steps):
        came_a.append(ga.advance(*(landed[k - 2] if k >= 2 else [])))
        landed.append([])
        for d in groups[k]:
            got[d] = cross(after(buckets[d], *came_a[k - 1]) if k else buckets[d], d)
            landed[k].append(got[d])
    ga.cores()
    mat_qkv, vectors = ga.matrices(me, [(0, wide, 1), (wide, block_width, 1)])
    devices = dp_size * peer_count
    here = ga.parts[2][:, :, wide - ga.bounds[1] :]
    slots = [cube.masks(slot, cube.far + cube.near[1]) for slot in range(here.shape[0])]
    dest_peers = [mask_f for mask_a, mask_f in slots if mask_a == 0]
    here = jnp.stack([here[i] for i, (mask_a, _) in enumerate(slots) if mask_a == 0])

    def rows_of(blocks, first, count):
        rows = [
            blocks[:, r % shard, (r // shard) * LANES : (r // shard + 1) * LANES]
            for r in range(first, first + count)
        ]
        return jnp.stack(rows, axis=1)

    def spread_lanes(values, size):
        lanes = lax.broadcasted_iota(jnp.int32, (LANES, size), 0)
        places = lax.broadcasted_iota(jnp.int32, (LANES, size), 1)
        return dot_nn(values, (places % shard == lanes).astype(BF16))

    vectors = vectors.reshape(devices, shard, block_width)
    flat = spread_lanes(rows_of(vectors, 0, 8).reshape(devices * 8, LANES), width)
    place = lax.broadcasted_iota(jnp.int32, (devices, 8, width), 2) // shard
    owner = lax.broadcasted_iota(jnp.int32, (devices, 8, width), 0)
    flat = jnp.sum(jnp.where(place == owner, flat.reshape(devices, 8, width), 0.0), axis=0)
    gain_one, shift_one, bias_q, bias_v, bias_out, gain_two, shift_two, bias_down = flat
    count = devices * spread
    flat = spread_lanes(rows_of(vectors, 9, spread).reshape(count, LANES), hidden)
    place = lax.broadcasted_iota(jnp.int32, (count, hidden), 1) // shard
    owner = lax.broadcasted_iota(jnp.int32, (count, hidden), 0)
    bias_up = jnp.sum(jnp.where(place == owner, flat, 0.0), axis=0)

    here = rows_of(here, 8, 1)[:, 0, :tile_count].astype(jnp.int32)
    wanted = my_fs * tile_count + jnp.arange(tile_count, dtype=jnp.int32)
    found = here[None] == wanted[:, None, None]
    dest_peers = jnp.array(dest_peers, dtype=jnp.int32)
    came_far = jnp.sum(jnp.where(found, dest_peers[None, :, None], 0), axis=(1, 2))
    origin = came_far ^ my_fs

    local_tokens = collect(
        "take_tokens", came_far, [got[d] for d in range(peer_count)], tile_count
    ).reshape(row_count, width)
    cot_buckets = deal(
        "deal_cotangent", target, after(cotangent.reshape(tiled), local_tokens), peer_count
    )
    got_cot = lax.all_to_all(cot_buckets, "fsdp", split_axis=0, concat_axis=0, tiled=True)

    segment, valid_rows = layout(seq_lengths[0], row_count, tile_rows)
    query_segment = segment[None, :]
    key_segment = jnp.where(valid_rows, segment, -1)[:, None]

    stream = local_tokens.astype(F32)
    hat_one, rho_one = normalize(stream)
    norm_one = (hat_one * gain_one + shift_one).astype(BF16)
    qkv_shift = jnp.concatenate([bias_q, jnp.zeros((width,), F32), bias_v])
    norm_one = after(norm_one, cot_buckets)
    qkv_low = (dot_nn(norm_one, mat_qkv) + qkv_shift).astype(BF16)
    attn_out, lse = attend_forward(
        qkv_low, query_segment, key_segment
    )
    mid_stream = stream + dot_nn(attn_out, mat_out) + bias_out
    hat_two, rho_two = normalize(mid_stream)
    norm_two = (hat_two * gain_two + shift_two).astype(BF16)
    pre_act = dot_nn(norm_two, mat_up) + bias_up
    norm_two = after(norm_two, got_cot)
    local_cot = deal("take_cotangent", origin, None, after(got_cot, norm_two))
    local_cot = local_cot.reshape(row_count, width)
    act_value, gelu_pull = jax.vjp(gelu_tanh, pre_act)
    act_low = lax.optimization_barrier(act_value.astype(BF16))
    result = (mid_stream + dot_nn(act_low, mat_down) + bias_down).astype(BF16)
    mixed_buckets = deal("return_mixed", origin, result.reshape(tiled), peer_count)
    got_mixed = lax.all_to_all(mixed_buckets, "fsdp", split_axis=0, concat_axis=0, tiled=True)

    grad_out_rows = local_cot.astype(F32) * valid_rows.astype(F32)[:, None]
    grad_out_low = after(grad_out_rows.astype(BF16), mixed_buckets)
    d_down_bias = col_sums(grad_out_low)
    d_w_down = dot_tn(act_low, grad_out_low).astype(BF16)
    s_down = lax.psum_scatter(d_w_down, AXES, scatter_dimension=0, tiled=True).astype(F32)

    d_act = dot_nt(after(grad_out_low, d_w_down), mat_down)
    d_pre = gelu_pull(d_act)[0].astype(BF16)

    d_up_bias = col_sums(d_pre)
    d_w_up = dot_tn(norm_two, d_pre).astype(BF16)
    d_norm_two = dot_nt(after(d_pre, d_w_up), mat_up)
    d_gain_two = jnp.sum(d_norm_two * hat_two, axis=0, keepdims=True)
    d_shift_two = jnp.sum(d_norm_two, axis=0, keepdims=True)
    d_mid = grad_out_rows + normalize_back(d_norm_two, gain_two, hat_two, rho_two)
    d_proj_low = d_mid.astype(BF16)
    d_out_bias = col_sums(d_proj_low)
    d_w_out = dot_tn(attn_out, d_proj_low).astype(BF16)
    give, keep = scatter_split(cube, me, [(d_w_up, 1), (d_w_out, 1)], shard)
    up = Scatter(cube, give, keep, (hidden + width) // 2)
    sent_up = up.start()
    d_attn = dot_nt(after(d_proj_low, give, got_mixed), mat_out).astype(BF16)

    d_qkv = attend_backward(qkv_low, d_attn, lse, query_segment, key_segment)
    up.finish(tied(sent_up, d_qkv))
    sent_up = up.start()
    d_qkv = after(d_qkv, *up.give)
    d_q_bias = col_sums(d_qkv[:, :width])
    d_v_bias = col_sums(d_qkv[:, 2 * width :])
    d_w_qkv = dot_tn(norm_one, d_qkv).astype(BF16)
    give, keep = scatter_split(cube, me, [(d_w_qkv, 1)], shard)
    qkv = Scatter(cube, give, keep, wide // 2)
    sent_qkv = qkv.start()
    d_norm_one = dot_nt(after(d_qkv, give), mat_qkv)
    d_gain_one = jnp.sum(d_norm_one * hat_one, axis=0, keepdims=True)
    d_shift_one = jnp.sum(d_norm_one, axis=0, keepdims=True)
    d_stream = d_mid + normalize_back(d_norm_one, gain_one, hat_one, rho_one)
    qkv.finish(tied(sent_qkv, d_norm_one))
    sent_qkv = qkv.start()

    tiles = after(d_stream.astype(BF16).reshape(tiled), *qkv.give)
    buckets = deal_apart("return_gradient", came_far, tiles, peer_count)

    d_small = [
        d_gain_one,
        d_shift_one,
        d_q_bias,
        d_v_bias,
        d_out_bias,
        d_gain_two,
        d_shift_two,
        d_down_bias,
    ]
    d_rows = d_small + [d_up_bias[:, j * width : (j + 1) * width] for j in range(spread)]
    value = jnp.concatenate(d_rows, axis=0)
    vector_links = [cube.core] + cube.near[0][::-1] + cube.far[::-1]

    up_pieces = [(0, hidden, 1), (hidden, width, 1)]
    got = {0: buckets[0]}
    s_qkv = s_up = None
    slack, moved = [], buckets
    k = 0
    while s_qkv is None or k < max(steps, len(vector_links)):
        started = []
        if k < steps:
            for d, bucket in zip(groups[k], tied([buckets[d] for d in groups[k]], *moved)):
                got[d] = cross(bucket, d)
                started.append(got[d])
        if k < len(vector_links):
            value = after(value, *moved)
            value = value + cube.swap(value, vector_links[k])
            started.append(value)
        if s_qkv is None:
            moved = sent_qkv
            s_qkv = qkv.finish(tied(sent_qkv, *slack), [(0, wide, 1)])
            if s_qkv is None:
                sent_qkv = qkv.start()
        if s_up is None:
            s_up = up.finish(tied(sent_up, *moved), up_pieces)
            if s_up is None:
                sent_up = up.start()
                started += sent_up
        slack = started
        k += 1
    while s_up is None:
        s_up = up.finish(sent_up, up_pieces)
        sent_up = up.start() if s_up is None else None
    s_rows = value
    grad_tokens = collect(
        "take_gradient", distance, [got[d] for d in range(peer_count)], tile_count
    ).reshape(row_count, width)
    mixed = deal("take_mixed", target, None, after(got_mixed, *buckets)).reshape(row_count, width)
    my_place = my_dp * peer_count + my_fs
    s_block = lax.dynamic_slice(s_rows, (0, my_place * shard), (8, shard))
    s_up_bias = lax.dynamic_slice(
        s_rows[8:].reshape(hidden), (my_place * hidden_shard,), (hidden_shard,)
    )

    return (
        mixed,
        grad_tokens,
        s_block[0],
        s_block[1],
        s_qkv[0],
        s_block[2],
        s_block[3],
        s_up[1],
        s_block[4],
        s_block[5],
        s_block[6],
        s_up[0],
        s_up_bias,
        s_down,
        s_block[7],
    )


def solution(mesh):
    rows, matrix = P(AXES), P(AXES, None)
    in_specs = (
        matrix,
        matrix,
        rows,
        matrix,
        rows,
        rows,
        matrix,
        rows,
        rows,
        matrix,
        rows,
        rows,
        rows,
        matrix,
        rows,
        matrix,
        rows,
    )
    out_specs = (
        matrix,
        matrix,
        rows,
        rows,
        matrix,
        rows,
        rows,
        matrix,
        rows,
        rows,
        rows,
        matrix,
        rows,
        matrix,
        rows,
    )
    return jax.shard_map(
        per_device, mesh=mesh, in_specs=in_specs, out_specs=out_specs, check_vma=False
    )
```

```python
import functools

import jax
import jax.numpy as jnp
from jax import lax
from jax.experimental import pallas as pl
from jax.experimental.pallas import tpu as pltpu
from jax.sharding import PartitionSpec as P

HEAD_DIM = 64
LANES = 128
SCALE = 0.125
EPSILON = 1e-06
MASKED = -1000000000.0
F32 = jnp.float32
BF16 = jnp.bfloat16
AXES = ("dp", "fsdp")
LIGHT = pl.CostEstimate(flops=0, transcendentals=0, bytes_accessed=0)


def bits_of(size):
    return size.bit_length() - 1


class Cube:
    def __init__(self, dp_size, fs_size):
        self.size = {"dp": dp_size, "fsdp": fs_size}
        self.dp_high, self.fs_size = dp_size // 2, fs_size
        high_dp = [("dp", b) for b in reversed(range(1, bits_of(dp_size)))]
        low_fs = [("fsdp", 0)]
        self.core = ("dp", 0)
        self.far = [("fsdp", b) for b in reversed(range(1, bits_of(fs_size)))]
        self.near = (high_dp + low_fs, low_fs + high_dp)
        self.natural = high_dp + self.far + low_fs

    def swap(self, value, link):
        axis, bit = link
        pairs = [(i, i ^ (1 << bit)) for i in range(self.size[axis])]
        return lax.ppermute(value, axis, pairs)

    def masks(self, slot, order):
        found = {"dp": 0, "fsdp": 0}
        for k, (axis, bit) in enumerate(order):
            found[axis] |= ((slot >> k) & 1) << bit
        return found["dp"] >> 1, found["fsdp"]


def move(name, scalars, sources, out_shapes, plan):
    count = len(sources)
    total = sum(2 * s.size * s.dtype.itemsize for s in out_shapes)

    def kernel(scalar_ref, *refs):
        srcs, outs = refs[:count], refs[count : count + len(out_shapes)]
        sems = refs[-1]
        copies = [
            pltpu.make_async_copy(src, out, sems.at[i])
            for i, (src, out) in enumerate(plan(scalar_ref, srcs, outs))
        ]
        for copy in copies:
            copy.start()
        for copy in copies:
            copy.wait()

    class Counter:
        def __getitem__(self, key):
            return jnp.int32(0)

    class Blank:
        @property
        def at(self):
            return self

        def __getitem__(self, key):
            return self

    copies = len(
        plan(Counter(), [Blank() for _ in sources], [Blank() for _ in out_shapes])
    )
    return pl.pallas_call(
        kernel,
        out_shape=out_shapes,
        in_specs=[pl.BlockSpec(memory_space=pltpu.SMEM)]
        + [pl.BlockSpec(memory_space=pl.ANY) for _ in sources],
        out_specs=[pl.BlockSpec(memory_space=pltpu.VMEM) for _ in out_shapes],
        scratch_shapes=[pltpu.SemaphoreType.DMA((copies,))],
        cost_estimate=LIGHT,
        name=name,
    )(scalars, *sources)


def after(value, *others):
    return lax.optimization_barrier((value,) + others)[0]


def tied(values, *others):
    if not others:
        return list(values)
    return list(lax.optimization_barrier(tuple(values) + others)[: len(values)])


class Gather:
    def __init__(self, cube, shard, cut):
        self.cube, self.bounds = cube, (0, cut, shard.shape[1])
        self.parts, self.moved = [shard[None]], []
        self.steps = [[link] for link in cube.far] + [list(pair) for pair in zip(*cube.near)]
        self.step = 0

    def advance(self, *others):
        links, count = self.steps[self.step], len(self.parts)
        parts = tied(self.parts + self.moved, *others)
        parts, moved = parts[:count], parts[count:]
        if moved:
            parts = [jnp.concatenate(pair, axis=0) for pair in zip(parts, moved)]
        if len(links) > len(parts):
            bounds = self.bounds
            parts = [lax.slice_in_dim(parts[0], bounds[i], bounds[i + 1], axis=2) for i in range(2)]
        self.parts = parts
        self.moved = [self.cube.swap(part, link) for part, link in zip(parts, links)]
        self.step += 1
        return self.moved

    def cores(self, *others):
        parts = tied(self.parts + self.moved, *others)
        self.parts = [parts[0], parts[2], parts[1], parts[3]]
        self.others = [self.cube.swap(part, self.cube.core) for part in self.parts]
        return self.others

    def matrices(self, me, pieces, *others):
        cube, bounds = self.cube, self.bounds
        half, rows = self.parts[0].shape[:2]

        def plan(me_ref, srcs, outs):
            core = me_ref[0] & 1
            pairs = []
            for i in range(2):
                order = cube.far + cube.near[i]
                for out, (first, wide, blocks) in zip(outs, pieces):
                    each = wide // blocks
                    for j in range(blocks):
                        low = max(bounds[i], first + j * each)
                        high = min(bounds[i + 1], first + (j + 1) * each)
                        if low >= high:
                            continue
                        taken = pl.ds(low - bounds[i], high - low)
                        placed = pl.ds(low - first - j * each, high - low)
                        for slot in range(2 * half):
                            mask_a, mask_f = cube.masks(slot, order)
                            a, f = (me_ref[0] >> 1) ^ mask_a, me_ref[1] ^ mask_f
                            for k in range(2):
                                src = srcs[4 * k + 2 * i + slot // half].at[slot % half, :, taken]
                                pairs.append((src, out.at[a, core ^ k, f, j, :, placed]))
            return pairs

        shapes = [
            jax.ShapeDtypeStruct(
                (cube.dp_high, 2, cube.fs_size, blocks, rows, wide // blocks), BF16
            )
            for _, wide, blocks in pieces
        ]
        sources = tied(self.parts + self.others, *others)
        outs = move("interleave", me, sources, shapes, plan)
        return [out.reshape(-1, out.shape[-1]) for out in outs]


def deal_apart(name, scalars, tiles, peer_count):
    count, shape = tiles.shape[0], tiles.shape[1:]

    def kernel(far_ref, src, *refs):
        outs, held, sems = refs[:peer_count], refs[-2], refs[-1]
        into = [pltpu.make_async_copy(src.at[i], held.at[i], sems.at[0, i]) for i in range(count)]
        for copy in into:
            copy.start()
        for i in range(count):
            into[i].wait()
            for d in range(peer_count):

                @pl.when(far_ref[i] == d)
                def _():
                    pltpu.make_async_copy(held.at[i], outs[d], sems.at[1, i]).start()

        for i in range(count):
            pltpu.make_async_copy(held.at[i], outs[0], sems.at[1, i]).wait()

    return pl.pallas_call(
        kernel,
        out_shape=[jax.ShapeDtypeStruct(shape, tiles.dtype)] * peer_count,
        in_specs=[pl.BlockSpec(memory_space=pltpu.SMEM), pl.BlockSpec(memory_space=pl.ANY)],
        out_specs=[pl.BlockSpec(memory_space=pl.ANY)] * peer_count,
        scratch_shapes=[
            pltpu.VMEM((count,) + shape, tiles.dtype),
            pltpu.SemaphoreType.DMA((2, count)),
        ],
        cost_estimate=LIGHT,
        name=name,
    )(scalars, tiles)


def collect(name, scalars, buckets, count):
    shape, dtype = buckets[0].shape, buckets[0].dtype
    peer_count = len(buckets)

    def kernel(far_ref, *refs):
        srcs, out, held, sems = refs[:peer_count], refs[peer_count], refs[-2], refs[-1]
        back = [pltpu.make_async_copy(held.at[i], out.at[i], sems.at[1, i]) for i in range(count)]
        for i in range(count):
            for d in range(peer_count):

                @pl.when(far_ref[i] == d)
                def _():
                    pltpu.make_async_copy(srcs[d], held.at[i], sems.at[0, i]).start()

        for i in range(count):
            pltpu.make_async_copy(srcs[0], held.at[i], sems.at[0, i]).wait()
            back[i].start()
        for copy in back:
            copy.wait()

    return pl.pallas_call(
        kernel,
        out_shape=jax.ShapeDtypeStruct((count,) + shape, dtype),
        in_specs=[pl.BlockSpec(memory_space=pltpu.SMEM)]
        + [pl.BlockSpec(memory_space=pl.ANY)] * peer_count,
        out_specs=pl.BlockSpec(memory_space=pl.ANY),
        scratch_shapes=[
            pltpu.VMEM((count,) + shape, dtype),
            pltpu.SemaphoreType.DMA((2, count)),
        ],
        cost_estimate=LIGHT,
        name=name,
    )(scalars, *buckets)


def deal_apart(name, scalars, tiles, peer_count):
    count, shape = tiles.shape[0], tiles.shape[1:]

    def kernel(far_ref, src, *refs):
        outs, held, sems = refs[:peer_count], refs[-2], refs[-1]
        into = [pltpu.make_async_copy(src.at[i], held.at[i], sems.at[0, i]) for i in range(count)]
        for copy in into:
            copy.start()
        for i in range(count):
            into[i].wait()
            for d in range(peer_count):

                @pl.when(far_ref[i] == d)
                def _():
                    pltpu.make_async_copy(held.at[i], outs[d], sems.at[1, i]).start()

        for i in range(count):
            pltpu.make_async_copy(held.at[i], outs[0], sems.at[1, i]).wait()

    return pl.pallas_call(
        kernel,
        out_shape=[jax.ShapeDtypeStruct(shape, tiles.dtype)] * peer_count,
        in_specs=[pl.BlockSpec(memory_space=pltpu.SMEM), pl.BlockSpec(memory_space=pl.ANY)],
        out_specs=[pl.BlockSpec(memory_space=pl.ANY)] * peer_count,
        scratch_shapes=[
            pltpu.VMEM((count,) + shape, tiles.dtype),
            pltpu.SemaphoreType.DMA((2, count)),
        ],
        cost_estimate=LIGHT,
        name=name,
    )(scalars, tiles)


def collect(name, scalars, buckets, count):
    shape, dtype = buckets[0].shape, buckets[0].dtype
    peer_count = len(buckets)

    def kernel(far_ref, *refs):
        srcs, out, held, sems = refs[:peer_count], refs[peer_count], refs[-2], refs[-1]
        back = [pltpu.make_async_copy(held.at[i], out.at[i], sems.at[1, i]) for i in range(count)]
        for i in range(count):
            for d in range(peer_count):

                @pl.when(far_ref[i] == d)
                def _():
                    pltpu.make_async_copy(srcs[d], held.at[i], sems.at[0, i]).start()

        for i in range(count):
            pltpu.make_async_copy(srcs[0], held.at[i], sems.at[0, i]).wait()
            back[i].start()
        for copy in back:
            copy.wait()

    return pl.pallas_call(
        kernel,
        out_shape=jax.ShapeDtypeStruct((count,) + shape, dtype),
        in_specs=[pl.BlockSpec(memory_space=pltpu.SMEM)]
        + [pl.BlockSpec(memory_space=pl.ANY)] * peer_count,
        out_specs=pl.BlockSpec(memory_space=pl.ANY),
        scratch_shapes=[
            pltpu.VMEM((count,) + shape, dtype),
            pltpu.SemaphoreType.DMA((2, count)),
        ],
        cost_estimate=LIGHT,
        name=name,
    )(scalars, *buckets)


def deal(name, peers, tiles, buckets):
    source = buckets if tiles is None else tiles
    count, shape = peers.shape[0], source.shape[1:]
    out_count = count if tiles is None else buckets

    def kernel(peers_ref, src, out, held, sems):
        into, back = [], []
        for i in range(count):
            peer = peers_ref[i]
            here, there = (peer, i) if tiles is None else (i, peer)
            into.append(pltpu.make_async_copy(src.at[here], held.at[i], sems.at[0, i]))
            back.append(pltpu.make_async_copy(held.at[i], out.at[there], sems.at[1, i]))
        for copy in into:
            copy.start()
        for first, second in zip(into, back):
            first.wait()
            second.start()
        for copy in back:
            copy.wait()

    return pl.pallas_call(
        kernel,
        out_shape=jax.ShapeDtypeStruct((out_count,) + shape, source.dtype),
        in_specs=[pl.BlockSpec(memory_space=pltpu.SMEM), pl.BlockSpec(memory_space=pl.ANY)],
        out_specs=pl.BlockSpec(memory_space=pl.ANY),
        scratch_shapes=[
            pltpu.VMEM((count,) + shape, source.dtype),
            pltpu.SemaphoreType.DMA((2, count)),
        ],
        cost_estimate=LIGHT,
        name=name,
    )(peers, source)


def weight_grads(cube, me, jobs, rows, blocks):
    slots = cube.dp_high * cube.fs_size
    order = cube.natural[::-1]
    tokens, height = jobs[0][0].shape
    columns = jobs[0][1].shape[1] if blocks > 1 else min(height, jobs[-1][1].shape[1])
    aligned = rows % 8 == 0
    counts = [right.shape[1] // columns for _, right in jobs]
    starts = [sum(counts[:i]) for i in range(len(jobs))]
    steps = sum(counts)

    def kernel(me_ref, *refs):
        lefts, rights = refs[0 : 2 * len(jobs) : 2], refs[1 : 2 * len(jobs) : 2]
        outs, product = refs[2 * len(jobs) : 2 * len(jobs) + 2], refs[-1]
        step = pl.program_id(0)
        for left, right, start, count in zip(lefts, rights, starts, counts):

            @pl.when((step >= start) & (step < start + count))
            def _():
                value = dot_tn(left[...], right[...])
                if aligned:
                    product[...] = value
                else:
                    for i in range(height // rows):
                        product[i] = value[i * rows : (i + 1) * rows]

        core = me_ref[0] & 1
        for slot in range(slots):
            mask_a, mask_f = cube.masks(slot, order)
            a, f = (me_ref[0] >> 1) ^ mask_a, me_ref[1] ^ mask_f
            for k, out in enumerate(outs):
                owner = (2 * a + (core ^ k)) * cube.fs_size + f
                for j in range(blocks):
                    piece = owner * blocks + j
                    if aligned:
                        value = product[pl.ds(pl.multiple_of(piece * rows, 8), rows), :]
                    else:
                        value = product[piece]
                    out[slot, :, j * columns : (j + 1) * columns] = value.astype(BF16)

    def column(start, count):
        return lambda i, me_ref: (0, jnp.clip(i - start, 0, count - 1))

    in_specs, operands = [], []
    for (left, right), start, count in zip(jobs, starts, counts):
        in_specs.append(pl.BlockSpec((tokens, height), lambda i, me_ref: (0, 0)))
        in_specs.append(pl.BlockSpec((tokens, columns), column(start, count)))
        operands += [left, right]
    shape = jax.ShapeDtypeStruct((slots, rows, steps * blocks * columns), BF16)
    keep, give = pl.pallas_call(
        kernel,
        out_shape=[shape, shape],
        grid_spec=pltpu.PrefetchScalarGridSpec(
            num_scalar_prefetch=1,
            grid=(steps,),
            in_specs=in_specs,
            out_specs=[
                pl.BlockSpec((slots, rows, blocks * columns), lambda i, me_ref: (0, 0, i))
            ]
            * 2,
            scratch_shapes=[
                pltpu.VMEM((height, columns) if aligned else (height // rows, rows, columns), F32)
            ],
        ),
        cost_estimate=LIGHT,
        name="weight_grads",
    )(me, *operands)
    return give, keep


class Scatter:
    def __init__(self, cube, give, keep, cut):
        self.cube, self.cut = cube, cut
        self.give, self.keep = [give], [keep]
        self.left = [cube.natural[::-1]]
        self.plan = [[cube.core]] + [list(pair) for pair in zip(cube.near[0][::-1], cube.near[1][::-1])]
        self.plan += [[link] for link in cube.far[::-1]]
        self.step = 0

    def start(self):
        links = self.plan[self.step]
        return [self.cube.swap(give, link) for give, link in zip(self.give, links)]

    def finish(self, got, pieces=None):
        self.step += 1
        rows = self.keep[0].shape[1]
        widths = [k.shape[2] for k in self.keep]
        copies = []
        if self.step == len(self.plan):
            shapes = [
                jax.ShapeDtypeStruct((blocks * rows, wide // blocks), F32)
                for _, wide, blocks in pieces
            ]
            for o, (first, wide, blocks) in enumerate(pieces):
                each = wide // blocks
                for j in range(blocks):
                    low = first + j * each
                    target = (slice(j * rows, (j + 1) * rows), slice(None))
                    copies.append((0, 0, slice(low, low + each), o, target))
            return self.add(got, shapes, copies)
        links = self.plan[self.step]
        if len(links) > len(widths):
            ranges = [(0, 0, self.cut, 0, 0), (0, self.cut, widths[0], 1, 0)]
            self.left = [self.left[0], list(self.left[0])]
            new_widths = [self.cut, widths[0] - self.cut]
        elif len(links) < len(widths):
            ranges = [(0, 0, widths[0], 0, 0), (1, 0, widths[1], 0, widths[0])]
            new_widths = [sum(widths)]
        else:
            ranges = [(i, 0, w, i, 0) for i, w in enumerate(widths)]
            new_widths = widths
        slots = self.keep[0].shape[0]
        for source, low, high, part, first in ranges:
            bit = self.left[part].index(links[part])
            for slot in range(slots):
                side, rest = (slot >> bit) & 1, (slot >> (bit + 1) << bit) | (slot & ((1 << bit) - 1))
                target = (rest, slice(None), slice(first, first + high - low))
                copies.append((source, slot, slice(low, high), 2 * part + side, target))
        shapes = [
            jax.ShapeDtypeStruct((slots // 2, rows, w), BF16) for w in new_widths for _ in range(2)
        ]
        outs = self.add(got, shapes, copies)
        self.keep, self.give = outs[0::2], outs[1::2]
        self.left = [
            [link for link in self.left[i] if link != links[i]] for i in range(len(links))
        ]
        return None

    def add(self, got, shapes, copies):
        count = len(got)
        if self.keep[0].shape[0] <= 2:
            rows = {}
            for source, slot, columns, o, target in copies:
                mine = self.keep[source][slot, :, columns].astype(F32)
                total = (mine + got[source][slot, :, columns].astype(F32)).astype(shapes[o].dtype)
                rows.setdefault(o, []).append(total)
            outs = []
            for o, shape in enumerate(shapes):
                value = rows[o][0] if len(rows[o]) == 1 else jnp.concatenate(rows[o], axis=0)
                outs.append(value.reshape(shape.shape))
            return outs

        def kernel(*refs):
            outs = refs[2 * count :]
            for source, slot, columns, o, target in copies:
                mine = refs[source][slot, :, columns].astype(F32)
                came = refs[count + source][slot, :, columns].astype(F32)
                outs[o][target] = (mine + came).astype(outs[o].dtype)

        total = sum(2 * v.size * 2 for v in self.keep)
        return pl.pallas_call(
            kernel,
            out_shape=shapes,
            in_specs=[pl.BlockSpec(memory_space=pltpu.VMEM)] * (2 * count),
            out_specs=[pl.BlockSpec(memory_space=pltpu.VMEM)] * len(shapes),
            cost_estimate=LIGHT,
            name="add_step",
        )(*self.keep, *got)


def dot_nn(left, right):
    return jnp.dot(left, right, preferred_element_type=F32)


def dot_tn(left, right):
    return lax.dot_general(left, right, (((0,), (0,)), ((), ())), preferred_element_type=F32)


def dot_nt(left, right):
    return lax.dot_general(left, right, (((1,), (1,)), ((), ())), preferred_element_type=F32)


def attend_forward(qkv, query_segment, key_segment):
    rows, width = qkv.shape
    width = width // 3
    blocks = width // LANES

    def kernel(q_ref, k_ref, v_ref, qs_ref, ks_ref, out_ref, lse_ref):
        allowed = ks_ref[...] == qs_ref[...]
        q = q_ref[...] * SCALE
        k = k_ref[...]
        v_t = v_ref[...].T
        lane = lax.broadcasted_iota(jnp.int32, (1, LANES), 1)
        outs = []
        for h in range(LANES // HEAD_DIM):
            k_h = jnp.where(lane // HEAD_DIM == h, k, jnp.zeros_like(k))
            scores = jnp.where(allowed, dot_nt(k_h, q), MASKED)
            top = jnp.max(scores, axis=0, keepdims=True)
            weight = jnp.exp(scores - top)
            total = jnp.sum(weight, axis=0, keepdims=True)
            probs = (weight * (1.0 / total)).astype(BF16)
            outs.append(dot_nn(v_t[h * HEAD_DIM : (h + 1) * HEAD_DIM], probs))
            lse_ref[0, h : h + 1, :] = top + jnp.log(total)
        out_ref[...] = jnp.concatenate(outs, axis=0).T.astype(BF16)

    return pl.pallas_call(
        kernel,
        out_shape=[
            jax.ShapeDtypeStruct((rows, width), BF16),
            jax.ShapeDtypeStruct((blocks, LANES // HEAD_DIM, rows), F32),
        ],
        grid=(blocks,),
        in_specs=[
            pl.BlockSpec((rows, LANES), lambda i: (0, i)),
            pl.BlockSpec((rows, LANES), lambda i: (0, blocks + i)),
            pl.BlockSpec((rows, LANES), lambda i: (0, 2 * blocks + i)),
            pl.BlockSpec((1, rows), lambda i: (0, 0)),
            pl.BlockSpec((rows, 1), lambda i: (0, 0)),
        ],
        out_specs=[
            pl.BlockSpec((rows, LANES), lambda i: (0, i)),
            pl.BlockSpec((1, LANES // HEAD_DIM, rows), lambda i: (i, 0, 0)),
        ],
        cost_estimate=LIGHT,
        name="attend_forward",
    )(qkv, qkv, qkv, query_segment, key_segment)


def attend_backward(qkv, d_attn, lse, query_segment, key_segment):
    rows, width = d_attn.shape
    blocks = width // LANES

    def kernel(q_ref, k_ref, v_ref, d_ref, lse_ref, qs_ref, ks_ref, out_ref):
        allowed = ks_ref[...] == qs_ref[...]
        q = q_ref[...] * SCALE
        k = k_ref[...]
        v = v_ref[...]
        d_out = d_ref[...]
        k_t = k.T
        lane = lax.broadcasted_iota(jnp.int32, (1, LANES), 1)
        d_q, d_k, d_v = [], 0.0, 0.0
        for h in range(LANES // HEAD_DIM):
            here = lane // HEAD_DIM == h
            zero = jnp.zeros_like(k)
            k_h = jnp.where(here, k, zero)
            scores = dot_nt(k_h, q)
            probs = jnp.where(allowed, jnp.exp(scores - lse_ref[0, h : h + 1, :]), 0.0)
            d_out_h = jnp.where(here, d_out, zero)
            d_v = d_v + dot_nn(probs.astype(BF16), d_out_h)
            d_probs = dot_nt(v, d_out_h)
            inner = jnp.sum(probs * d_probs, axis=0, keepdims=True)
            d_scores = (probs * (d_probs - inner)).astype(BF16)
            d_k = d_k + dot_nn(d_scores, jnp.where(here, q, zero))
            d_q.append(dot_nn(k_t[h * HEAD_DIM : (h + 1) * HEAD_DIM], d_scores))
        d_q = jnp.concatenate(d_q, axis=0).T * SCALE
        for part, value in enumerate((d_q, d_k, d_v)):
            place = pl.multiple_of((pl.program_id(0) + part * blocks) * LANES, LANES)
            out_ref[:, pl.ds(place, LANES)] = value.astype(BF16)

    return pl.pallas_call(
        kernel,
        out_shape=jax.ShapeDtypeStruct((rows, 3 * width), BF16),
        grid=(blocks,),
        in_specs=[
            pl.BlockSpec((rows, LANES), lambda i: (0, i)),
            pl.BlockSpec((rows, LANES), lambda i: (0, blocks + i)),
            pl.BlockSpec((rows, LANES), lambda i: (0, 2 * blocks + i)),
            pl.BlockSpec((rows, LANES), lambda i: (0, i)),
            pl.BlockSpec((1, LANES // HEAD_DIM, rows), lambda i: (i, 0, 0)),
            pl.BlockSpec((1, rows), lambda i: (0, 0)),
            pl.BlockSpec((rows, 1), lambda i: (0, 0)),
        ],
        out_specs=pl.BlockSpec((rows, 3 * width), lambda i: (0, 0)),
        cost_estimate=LIGHT,
        name="attend_backward",
    )(qkv, qkv, qkv, d_attn, lse, query_segment, key_segment)


def normalize(stream):
    middle = jnp.mean(stream, axis=-1, keepdims=True)
    centered = stream - middle
    spread = jnp.mean(centered * centered, axis=-1, keepdims=True)
    rho = lax.rsqrt(spread + EPSILON)
    return centered * rho, rho


def normalize_back(grad, gain, hat, rho):
    scaled = grad * gain
    return rho * (
        scaled
        - jnp.mean(scaled, axis=-1, keepdims=True)
        - hat * jnp.mean(scaled * hat, axis=-1, keepdims=True)
    )


def gelu_tanh(values):
    return jax.nn.gelu(values, approximate=True)


def layout(lengths, row_count, tile_rows):
    tile_counts = (lengths + tile_rows - 1) // tile_rows
    seg_ends = jnp.cumsum(tile_counts) * tile_rows
    seg_starts = seg_ends - tile_counts * tile_rows
    position = jnp.arange(row_count, dtype=jnp.int32)[:, None]
    inside = (position >= seg_starts[None, :]) & (position < seg_ends[None, :])
    segment = jnp.sum((position >= seg_ends[None, :]).astype(jnp.int32), axis=1)
    offset = jnp.sum(jnp.where(inside, position - seg_starts[None, :], 0), axis=1)
    length_here = jnp.sum(jnp.where(inside, lengths[None, :], 0), axis=1)
    return (segment, offset < length_here)


def col_sums(values):
    return jnp.sum(values.astype(F32), axis=0, keepdims=True)


def per_device(
    tokens,
    cotangent,
    tile_dest,
    seq_lengths,
    norm1_gain,
    norm1_bias,
    w_qkv,
    q_bias,
    v_bias,
    w_out,
    out_bias,
    norm2_gain,
    norm2_bias,
    w_up,
    up_bias,
    w_down,
    down_bias,
):
    dp_size = lax.axis_size("dp")
    peer_count = lax.axis_size("fsdp")
    cube = Cube(dp_size, peer_count)
    my_dp, my_fs = lax.axis_index("dp"), lax.axis_index("fsdp")
    me = jnp.stack([my_dp, my_fs]).astype(jnp.int32)
    tile_count = tile_dest.shape[0]
    row_count, width = tokens.shape
    tile_rows = row_count // tile_count
    shard = w_qkv.shape[0]
    hidden = w_up.shape[1]
    hidden_shard = w_down.shape[0]
    spread = hidden // width

    small = [norm1_gain, norm1_bias, q_bias, v_bias, out_bias, norm2_gain, norm2_bias, down_bias]
    dest_row = jnp.pad(tile_dest.astype(F32), (0, shard - tile_count))
    block = jnp.concatenate(
        [v.reshape(1, shard) for v in small + [dest_row]] + [up_bias.reshape(spread, shard)], axis=0
    )
    block_rows = block.shape[0]
    groups = -(-block_rows // shard)
    block = jnp.pad(block, ((0, groups * shard - block_rows), (0, LANES - shard)))
    if groups > 1:
        block = jnp.concatenate(jnp.split(block, groups, axis=0), axis=1)
    block_width = groups * LANES
    target = tile_dest // tile_count
    tiled = (tile_count, tile_rows, width)
    bucketed = (peer_count, tile_rows, width)

    wide = 3 * width
    half = hidden // 2
    chunk_a = jnp.concatenate([w_qkv, block], axis=1).astype(BF16)
    pieces = [w_out] + [w_up[:, j * width : (j + 1) * width] for j in range(spread)] + [w_down]
    chunk_b = jnp.concatenate([p.astype(BF16) for p in pieces], axis=0)
    full = lax.all_gather(chunk_b, AXES, axis=0, tiled=False)
    mat_out = full[:, :shard].reshape(-1, width)
    mat_up = jnp.concatenate(
        [full[:, (1 + j) * shard : (2 + j) * shard].reshape(-1, width) for j in range(spread)], axis=1
    )
    mat_down = full[:, (1 + spread) * shard :].reshape(hidden, width)
    distance = target ^ my_fs
    token_tiles = after(tokens.reshape(tiled), chunk_a)
    buckets = deal_apart("deal_tokens", distance, token_tiles, peer_count)

    def cross(bucket, d):
        return lax.ppermute(bucket, "fsdp", [(i, i ^ d) for i in range(peer_count)])

    cut_a = (chunk_a.shape[1] // 2 + LANES - 1) // LANES * LANES
    ga = Gather(cube, chunk_a, cut_a)
    steps = len(ga.steps)
    far = sorted(range(peer_count // 2, peer_count), key=lambda d: (d & 1, d))
    near = list(range(1, peer_count // 2))
    groups = [far[k::steps] + near[k::steps] for k in range(steps)]
    got = {0: buckets[0]}
    came_a, landed = [], []
    for k in range(steps):
        came_a.append(ga.advance(*(landed[k - 2] if k >= 2 else [])))
        landed.append([])
        for d in groups[k]:
            got[d] = cross(after(buckets[d], *came_a[k - 1]) if k else buckets[d], d)
            landed[k].append(got[d])
    ga.cores()
    mat_qkv, vectors = ga.matrices(me, [(0, wide, 1), (wide, block_width, 1)])
    devices = dp_size * peer_count
    here = ga.parts[2][:, :, wide - ga.bounds[1] :]
    slots = [cube.masks(slot, cube.far + cube.near[1]) for slot in range(here.shape[0])]
    dest_peers = [mask_f for mask_a, mask_f in slots if mask_a == 0]
    here = jnp.stack([here[i] for i, (mask_a, _) in enumerate(slots) if mask_a == 0])

    def rows_of(blocks, first, count):
        rows = [
            blocks[:, r % shard, (r // shard) * LANES : (r // shard + 1) * LANES]
            for r in range(first, first + count)
        ]
        return jnp.stack(rows, axis=1)

    def spread_lanes(values, size):
        lanes = lax.broadcasted_iota(jnp.int32, (LANES, size), 0)
        places = lax.broadcasted_iota(jnp.int32, (LANES, size), 1)
        return dot_nn(values, (places % shard == lanes).astype(BF16))

    vectors = vectors.reshape(devices, shard, block_width)
    flat = spread_lanes(rows_of(vectors, 0, 8).reshape(devices * 8, LANES), width)
    place = lax.broadcasted_iota(jnp.int32, (devices, 8, width), 2) // shard
    owner = lax.broadcasted_iota(jnp.int32, (devices, 8, width), 0)
    flat = jnp.sum(jnp.where(place == owner, flat.reshape(devices, 8, width), 0.0), axis=0)
    gain_one, shift_one, bias_q, bias_v, bias_out, gain_two, shift_two, bias_down = flat
    count = devices * spread
    flat = spread_lanes(rows_of(vectors, 9, spread).reshape(count, LANES), hidden)
    place = lax.broadcasted_iota(jnp.int32, (count, hidden), 1) // shard
    owner = lax.broadcasted_iota(jnp.int32, (count, hidden), 0)
    bias_up = jnp.sum(jnp.where(place == owner, flat, 0.0), axis=0)

    here = rows_of(here, 8, 1)[:, 0, :tile_count].astype(jnp.int32)
    wanted = my_fs * tile_count + jnp.arange(tile_count, dtype=jnp.int32)
    found = here[None] == wanted[:, None, None]
    dest_peers = jnp.array(dest_peers, dtype=jnp.int32)
    came_far = jnp.sum(jnp.where(found, dest_peers[None, :, None], 0), axis=(1, 2))
    origin = came_far ^ my_fs

    local_tokens = collect(
        "take_tokens", came_far, [got[d] for d in range(peer_count)], tile_count
    ).reshape(row_count, width)
    cot_buckets = deal(
        "deal_cotangent", target, after(cotangent.reshape(tiled), local_tokens), peer_count
    )
    segment, valid_rows = layout(seq_lengths[0], row_count, tile_rows)
    query_segment = segment[None, :]
    key_segment = jnp.where(valid_rows, segment, -1)[:, None]

    stream = local_tokens.astype(F32)
    hat_one, rho_one = normalize(stream)
    norm_one = (hat_one * gain_one + shift_one).astype(BF16)
    qkv_shift = jnp.concatenate([bias_q, jnp.zeros((width,), F32), bias_v])
    norm_one = after(norm_one, cot_buckets)
    qkv_low = (dot_nn(norm_one, mat_qkv) + qkv_shift).astype(BF16)
    got_cot = lax.all_to_all(
        after(cot_buckets, qkv_low), "fsdp", split_axis=0, concat_axis=0, tiled=True
    )
    attn_out, lse = attend_forward(qkv_low, query_segment, key_segment)
    mid_stream = stream + dot_nn(attn_out, mat_out) + bias_out
    hat_two, rho_two = normalize(mid_stream)
    norm_two = (hat_two * gain_two + shift_two).astype(BF16)
    pre_act = dot_nn(norm_two, mat_up) + bias_up
    act_value, gelu_pull = jax.vjp(gelu_tanh, pre_act)
    act_low = lax.optimization_barrier(act_value.astype(BF16))
    result = (mid_stream + dot_nn(act_low, mat_down) + bias_down).astype(BF16)
    mixed_buckets = deal("return_mixed", origin, result.reshape(tiled), peer_count)
    got_mixed = lax.all_to_all(mixed_buckets, "fsdp", split_axis=0, concat_axis=0, tiled=True)

    local_cot = deal("take_cotangent", origin, None, after(got_cot, mixed_buckets))
    local_cot = local_cot.reshape(row_count, width)
    grad_out_rows = local_cot.astype(F32) * valid_rows.astype(F32)[:, None]
    grad_out_low = after(grad_out_rows.astype(BF16), mixed_buckets)
    d_down_bias = col_sums(grad_out_low)
    d_w_down = dot_tn(act_low, grad_out_low).astype(BF16)
    sum_down = lax.psum_scatter(d_w_down, AXES, scatter_dimension=0, tiled=True)

    d_act = dot_nt(after(grad_out_low, d_w_down), mat_down)
    d_pre = gelu_pull(d_act)[0].astype(BF16)

    d_up_bias = col_sums(d_pre)
    d_norm_two = dot_nt(d_pre, mat_up)
    d_gain_two = jnp.sum(d_norm_two * hat_two, axis=0, keepdims=True)
    d_shift_two = jnp.sum(d_norm_two, axis=0, keepdims=True)
    d_mid = grad_out_rows + normalize_back(d_norm_two, gain_two, hat_two, rho_two)
    d_proj_low = d_mid.astype(BF16)
    d_out_bias = col_sums(d_proj_low)
    give, keep = weight_grads(cube, me, [(norm_two, d_pre), (attn_out, d_proj_low)], shard, 1)
    up = Scatter(cube, give, keep, (hidden + width) // 2)
    sent_up = up.start()
    d_attn = dot_nt(after(d_proj_low, give, got_mixed), mat_out).astype(BF16)

    up.finish(tied(sent_up, d_attn))
    sent_up = up.start()
    d_attn = after(d_attn, *up.give)
    d_qkv = attend_backward(qkv_low, d_attn, lse, query_segment, key_segment)
    up.finish(tied(sent_up, d_qkv))
    sent_up = up.start()
    d_qkv = after(d_qkv, *up.give)
    d_q_bias = col_sums(d_qkv[:, :width])
    d_v_bias = col_sums(d_qkv[:, 2 * width :])
    give, keep = weight_grads(cube, me, [(norm_one, d_qkv)], shard, 1)
    qkv = Scatter(cube, give, keep, wide // 2)
    sent_qkv = qkv.start()
    d_norm_one = dot_nt(after(d_qkv, give), mat_qkv)
    d_gain_one = jnp.sum(d_norm_one * hat_one, axis=0, keepdims=True)
    d_shift_one = jnp.sum(d_norm_one, axis=0, keepdims=True)
    d_stream = d_mid + normalize_back(d_norm_one, gain_one, hat_one, rho_one)
    qkv.finish(tied(sent_qkv, d_norm_one))
    sent_qkv = qkv.start()

    tiles = after(d_stream.astype(BF16).reshape(tiled), *qkv.give, *sent_up)
    buckets = deal_apart("return_gradient", came_far, tiles, peer_count)

    d_small = [
        d_gain_one,
        d_shift_one,
        d_q_bias,
        d_v_bias,
        d_out_bias,
        d_gain_two,
        d_shift_two,
        d_down_bias,
    ]
    d_rows = d_small + [d_up_bias[:, j * width : (j + 1) * width] for j in range(spread)]
    value = jnp.concatenate(d_rows, axis=0)
    vector_links = [cube.core] + cube.near[0][::-1] + cube.far[::-1]

    vector_links = [cube.core] + cube.near[0][::-1] + cube.far[::-1]
    up_pieces = [(0, hidden, 1), (hidden, width, 1)]
    got = {0: buckets[0]}
    first = [d for d in far + near if not d & 1]
    second = [d for d in far + near if d & 1]
    waits = [first[:1], first[1:], second[:2], second[2:]]
    for d in first:
        got[d] = cross(buckets[d], d)
    s_qkv = s_up = None
    value = value + cube.swap(value, vector_links[0])
    moved, k = list(buckets), 0
    while s_qkv is None or k + 1 < len(vector_links):
        due = list(moved)
        if k < len(waits):
            due += [got[d] for d in waits[k]]
        if k == 0:
            due.append(sum_down)
        if s_qkv is None:
            came = tied(sent_qkv, *due)
            s_qkv = qkv.finish(came, [(0, wide, 1)])
            if s_qkv is None:
                sent_qkv = qkv.start()
        if k + 1 < len(vector_links):
            value = after(value, *moved)
            value = value + cube.swap(value, vector_links[k + 1])
        moved = came
        if s_up is None:
            s_up = up.finish(tied(sent_up, *moved), up_pieces)
            if s_up is None:
                sent_up = up.start()
        if k == 0:
            for d, bucket in zip(second, tied([buckets[d] for d in second], *moved)):
                got[d] = cross(bucket, d)
        k += 1
    s_rows = value
    grad_tokens = collect(
        "take_gradient", distance, [got[d] for d in range(peer_count)], tile_count
    ).reshape(row_count, width)
    mixed = deal("take_mixed", target, None, after(got_mixed, *buckets)).reshape(row_count, width)
    my_place = my_dp * peer_count + my_fs
    s_block = lax.dynamic_slice(s_rows, (0, my_place * shard), (8, shard))
    s_up_bias = lax.dynamic_slice(
        s_rows[8:].reshape(hidden), (my_place * hidden_shard,), (hidden_shard,)
    )

    return (
        mixed,
        grad_tokens,
        s_block[0],
        s_block[1],
        s_qkv[0],
        s_block[2],
        s_block[3],
        s_up[1],
        s_block[4],
        s_block[5],
        s_block[6],
        s_up[0],
        s_up_bias,
        sum_down.astype(F32),
        s_block[7],
    )


def solution(mesh):
    rows, matrix = P(AXES), P(AXES, None)
    in_specs = (
        matrix,
        matrix,
        rows,
        matrix,
        rows,
        rows,
        matrix,
        rows,
        rows,
        matrix,
        rows,
        rows,
        rows,
        matrix,
        rows,
        matrix,
        rows,
    )
    out_specs = (
        matrix,
        matrix,
        rows,
        rows,
        matrix,
        rows,
        rows,
        matrix,
        rows,
        rows,
        rows,
        matrix,
        rows,
        matrix,
        rows,
    )
    return jax.shard_map(
        per_device, mesh=mesh, in_specs=in_specs, out_specs=out_specs, check_vma=False
    )
```

```python
import math

import jax
import jax.numpy as jnp
from jax import lax
from jax.experimental import pallas as pl
from jax.experimental.pallas import tpu as pltpu
from jax.sharding import PartitionSpec as P

HEAD_DIM = 64
LANES = 128
SCALE = 0.125
EPSILON = 1e-06
MASKED = -1000000000.0
F32 = jnp.float32
BF16 = jnp.bfloat16
AXES = ("dp", "fsdp")
LIGHT = pl.CostEstimate(flops=0, transcendentals=0, bytes_accessed=0)


def bits_of(size):
    return size.bit_length() - 1


class Cube:
    def __init__(self, dp_size, fs_size):
        self.size = {"dp": dp_size, "fsdp": fs_size}
        self.dp_high, self.fs_size = dp_size // 2, fs_size
        high_dp = [("dp", b) for b in reversed(range(1, bits_of(dp_size)))]
        low_fs = [("fsdp", 0)]
        self.core = ("dp", 0)
        self.far = [("fsdp", b) for b in reversed(range(1, bits_of(fs_size)))]
        self.near = (high_dp + low_fs, low_fs + high_dp)
        self.natural = high_dp + self.far + low_fs

    def swap(self, value, link):
        axis, bit = link
        pairs = [(i, i ^ (1 << bit)) for i in range(self.size[axis])]
        return lax.ppermute(value, axis, pairs)

    def masks(self, slot, order):
        found = {"dp": 0, "fsdp": 0}
        for k, (axis, bit) in enumerate(order):
            found[axis] |= ((slot >> k) & 1) << bit
        return found["dp"] >> 1, found["fsdp"]


def move(name, scalars, sources, out_shapes, plan):
    count = len(sources)
    total = sum(2 * s.size * s.dtype.itemsize for s in out_shapes)

    def kernel(scalar_ref, *refs):
        srcs, outs = refs[:count], refs[count : count + len(out_shapes)]
        sems = refs[-1]
        copies = [
            pltpu.make_async_copy(src, out, sems.at[i])
            for i, (src, out) in enumerate(plan(scalar_ref, srcs, outs))
        ]
        for copy in copies:
            copy.start()
        for copy in copies:
            copy.wait()

    class Counter:
        def __getitem__(self, key):
            return jnp.int32(0)

    class Blank:
        @property
        def at(self):
            return self

        def __getitem__(self, key):
            return self

    copies = len(
        plan(Counter(), [Blank() for _ in sources], [Blank() for _ in out_shapes])
    )
    return pl.pallas_call(
        kernel,
        out_shape=out_shapes,
        in_specs=[pl.BlockSpec(memory_space=pltpu.SMEM)]
        + [pl.BlockSpec(memory_space=pl.ANY) for _ in sources],
        out_specs=[pl.BlockSpec(memory_space=pltpu.VMEM) for _ in out_shapes],
        scratch_shapes=[pltpu.SemaphoreType.DMA((copies,))],
        cost_estimate=LIGHT,
        name=name,
    )(scalars, *sources)


def after(value, *others):
    return lax.optimization_barrier((value,) + others)[0]


def tied(values, *others):
    if not others:
        return list(values)
    return list(lax.optimization_barrier(tuple(values) + others)[: len(values)])


class Gather:
    def __init__(self, cube, shard, cut):
        self.cube, self.bounds = cube, (0, cut, shard.shape[1])
        self.parts, self.moved = [shard[None]], []
        self.steps = [[link] for link in cube.far] + [list(pair) for pair in zip(*cube.near)]
        self.step = 0

    def advance(self, *others):
        links, count = self.steps[self.step], len(self.parts)
        parts = tied(self.parts + self.moved, *others)
        parts, moved = parts[:count], parts[count:]
        if moved:
            parts = [jnp.concatenate(pair, axis=0) for pair in zip(parts, moved)]
        if len(links) > len(parts):
            bounds = self.bounds
            parts = [lax.slice_in_dim(parts[0], bounds[i], bounds[i + 1], axis=2) for i in range(2)]
        self.parts = parts
        self.moved = [self.cube.swap(part, link) for part, link in zip(parts, links)]
        self.step += 1
        return self.moved

    def cores(self, *others):
        parts = tied(self.parts + self.moved, *others)
        self.parts = [parts[0], parts[2], parts[1], parts[3]]
        self.others = [self.cube.swap(part, self.cube.core) for part in self.parts]
        return self.others

    def matrices(self, me, pieces, *others):
        cube, bounds = self.cube, self.bounds
        half, rows = self.parts[0].shape[:2]

        def plan(me_ref, srcs, outs):
            core = me_ref[0] & 1
            pairs = []
            for i in range(2):
                order = cube.far + cube.near[i]
                for out, (first, wide, blocks) in zip(outs, pieces):
                    each = wide // blocks
                    for j in range(blocks):
                        low = max(bounds[i], first + j * each)
                        high = min(bounds[i + 1], first + (j + 1) * each)
                        if low >= high:
                            continue
                        taken = pl.ds(low - bounds[i], high - low)
                        placed = pl.ds(low - first - j * each, high - low)
                        for slot in range(2 * half):
                            mask_a, mask_f = cube.masks(slot, order)
                            a, f = (me_ref[0] >> 1) ^ mask_a, me_ref[1] ^ mask_f
                            for k in range(2):
                                src = srcs[4 * k + 2 * i + slot // half].at[slot % half, :, taken]
                                pairs.append((src, out.at[a, core ^ k, f, j, :, placed]))
            return pairs

        shapes = [
            jax.ShapeDtypeStruct(
                (cube.dp_high, 2, cube.fs_size, blocks, rows, wide // blocks), BF16
            )
            for _, wide, blocks in pieces
        ]
        sources = tied(self.parts + self.others, *others)
        outs = move("interleave", me, sources, shapes, plan)
        return [out.reshape(-1, out.shape[-1]) for out in outs]


def deal_apart(name, scalars, tiles, peer_count):
    count, shape = tiles.shape[0], tiles.shape[1:]

    def kernel(far_ref, src, *refs):
        outs, held, sems = refs[:peer_count], refs[-2], refs[-1]
        into = [pltpu.make_async_copy(src.at[i], held.at[i], sems.at[0, i]) for i in range(count)]
        for copy in into:
            copy.start()
        for i in range(count):
            into[i].wait()
            for d in range(peer_count):

                @pl.when(far_ref[i] == d)
                def _():
                    pltpu.make_async_copy(held.at[i], outs[d], sems.at[1, i]).start()

        for i in range(count):
            pltpu.make_async_copy(held.at[i], outs[0], sems.at[1, i]).wait()

    return pl.pallas_call(
        kernel,
        out_shape=[jax.ShapeDtypeStruct(shape, tiles.dtype)] * peer_count,
        in_specs=[pl.BlockSpec(memory_space=pltpu.SMEM), pl.BlockSpec(memory_space=pl.ANY)],
        out_specs=[pl.BlockSpec(memory_space=pl.ANY)] * peer_count,
        scratch_shapes=[
            pltpu.VMEM((count,) + shape, tiles.dtype),
            pltpu.SemaphoreType.DMA((2, count)),
        ],
        cost_estimate=LIGHT,
        name=name,
    )(scalars, tiles)


def collect(name, scalars, buckets, count):
    shape, dtype = buckets[0].shape, buckets[0].dtype
    peer_count = len(buckets)

    def kernel(far_ref, *refs):
        srcs, out, held, sems = refs[:peer_count], refs[peer_count], refs[-2], refs[-1]
        back = [pltpu.make_async_copy(held.at[i], out.at[i], sems.at[1, i]) for i in range(count)]
        for i in range(count):
            for d in range(peer_count):

                @pl.when(far_ref[i] == d)
                def _():
                    pltpu.make_async_copy(srcs[d], held.at[i], sems.at[0, i]).start()

        for i in range(count):
            pltpu.make_async_copy(srcs[0], held.at[i], sems.at[0, i]).wait()
            back[i].start()
        for copy in back:
            copy.wait()

    return pl.pallas_call(
        kernel,
        out_shape=jax.ShapeDtypeStruct((count,) + shape, dtype),
        in_specs=[pl.BlockSpec(memory_space=pltpu.SMEM)]
        + [pl.BlockSpec(memory_space=pl.ANY)] * peer_count,
        out_specs=pl.BlockSpec(memory_space=pl.ANY),
        scratch_shapes=[
            pltpu.VMEM((count,) + shape, dtype),
            pltpu.SemaphoreType.DMA((2, count)),
        ],
        cost_estimate=LIGHT,
        name=name,
    )(scalars, *buckets)


def deal_apart(name, scalars, tiles, peer_count):
    count, shape = tiles.shape[0], tiles.shape[1:]

    def kernel(far_ref, src, *refs):
        outs, held, sems = refs[:peer_count], refs[-2], refs[-1]
        into = [pltpu.make_async_copy(src.at[i], held.at[i], sems.at[0, i]) for i in range(count)]
        for copy in into:
            copy.start()
        for i in range(count):
            into[i].wait()
            for d in range(peer_count):

                @pl.when(far_ref[i] == d)
                def _():
                    pltpu.make_async_copy(held.at[i], outs[d], sems.at[1, i]).start()

        for i in range(count):
            pltpu.make_async_copy(held.at[i], outs[0], sems.at[1, i]).wait()

    return pl.pallas_call(
        kernel,
        out_shape=[jax.ShapeDtypeStruct(shape, tiles.dtype)] * peer_count,
        in_specs=[pl.BlockSpec(memory_space=pltpu.SMEM), pl.BlockSpec(memory_space=pl.ANY)],
        out_specs=[pl.BlockSpec(memory_space=pl.ANY)] * peer_count,
        scratch_shapes=[
            pltpu.VMEM((count,) + shape, tiles.dtype),
            pltpu.SemaphoreType.DMA((2, count)),
        ],
        cost_estimate=LIGHT,
        name=name,
    )(scalars, tiles)


def collect(name, scalars, buckets, count):
    shape, dtype = buckets[0].shape, buckets[0].dtype
    peer_count = len(buckets)

    def kernel(far_ref, *refs):
        srcs, out, held, sems = refs[:peer_count], refs[peer_count], refs[-2], refs[-1]
        back = [pltpu.make_async_copy(held.at[i], out.at[i], sems.at[1, i]) for i in range(count)]
        for i in range(count):
            for d in range(peer_count):

                @pl.when(far_ref[i] == d)
                def _():
                    pltpu.make_async_copy(srcs[d], held.at[i], sems.at[0, i]).start()

        for i in range(count):
            pltpu.make_async_copy(srcs[0], held.at[i], sems.at[0, i]).wait()
            back[i].start()
        for copy in back:
            copy.wait()

    return pl.pallas_call(
        kernel,
        out_shape=jax.ShapeDtypeStruct((count,) + shape, dtype),
        in_specs=[pl.BlockSpec(memory_space=pltpu.SMEM)]
        + [pl.BlockSpec(memory_space=pl.ANY)] * peer_count,
        out_specs=pl.BlockSpec(memory_space=pl.ANY),
        scratch_shapes=[
            pltpu.VMEM((count,) + shape, dtype),
            pltpu.SemaphoreType.DMA((2, count)),
        ],
        cost_estimate=LIGHT,
        name=name,
    )(scalars, *buckets)


def deal(name, peers, tiles, buckets):
    source = buckets if tiles is None else tiles
    count, shape = peers.shape[0], source.shape[1:]
    out_count = count if tiles is None else buckets

    def kernel(peers_ref, src, out, held, sems):
        into, back = [], []
        for i in range(count):
            peer = peers_ref[i]
            here, there = (peer, i) if tiles is None else (i, peer)
            into.append(pltpu.make_async_copy(src.at[here], held.at[i], sems.at[0, i]))
            back.append(pltpu.make_async_copy(held.at[i], out.at[there], sems.at[1, i]))
        for copy in into:
            copy.start()
        for first, second in zip(into, back):
            first.wait()
            second.start()
        for copy in back:
            copy.wait()

    return pl.pallas_call(
        kernel,
        out_shape=jax.ShapeDtypeStruct((out_count,) + shape, source.dtype),
        in_specs=[pl.BlockSpec(memory_space=pltpu.SMEM), pl.BlockSpec(memory_space=pl.ANY)],
        out_specs=pl.BlockSpec(memory_space=pl.ANY),
        scratch_shapes=[
            pltpu.VMEM((count,) + shape, source.dtype),
            pltpu.SemaphoreType.DMA((2, count)),
        ],
        cost_estimate=LIGHT,
        name=name,
    )(peers, source)


def weight_grads(cube, me, jobs, rows, blocks):
    slots = cube.dp_high * cube.fs_size
    order = cube.natural[::-1]
    tokens, height = jobs[0][0].shape
    columns = jobs[0][1].shape[1] if blocks > 1 else min(height, jobs[-1][1].shape[1])
    aligned = rows % 8 == 0
    counts = [right.shape[1] // columns for _, right in jobs]
    starts = [sum(counts[:i]) for i in range(len(jobs))]
    steps = sum(counts)

    def kernel(me_ref, *refs):
        lefts, rights = refs[0 : 2 * len(jobs) : 2], refs[1 : 2 * len(jobs) : 2]
        outs, product = refs[2 * len(jobs) : 2 * len(jobs) + 2], refs[-1]
        step = pl.program_id(0)
        for left, right, start, count in zip(lefts, rights, starts, counts):

            @pl.when((step >= start) & (step < start + count))
            def _():
                value = dot_tn(left[...], right[...])
                if aligned:
                    product[...] = value
                else:
                    for i in range(height // rows):
                        product[i] = value[i * rows : (i + 1) * rows]

        core = me_ref[0] & 1
        for slot in range(slots):
            mask_a, mask_f = cube.masks(slot, order)
            a, f = (me_ref[0] >> 1) ^ mask_a, me_ref[1] ^ mask_f
            for k, out in enumerate(outs):
                owner = (2 * a + (core ^ k)) * cube.fs_size + f
                for j in range(blocks):
                    piece = owner * blocks + j
                    if aligned:
                        value = product[pl.ds(pl.multiple_of(piece * rows, 8), rows), :]
                    else:
                        value = product[piece]
                    out[slot, :, j * columns : (j + 1) * columns] = value.astype(BF16)

    def column(start, count):
        return lambda i, me_ref: (0, jnp.clip(i - start, 0, count - 1))

    in_specs, operands = [], []
    for (left, right), start, count in zip(jobs, starts, counts):
        in_specs.append(pl.BlockSpec((tokens, height), lambda i, me_ref: (0, 0)))
        in_specs.append(pl.BlockSpec((tokens, columns), column(start, count)))
        operands += [left, right]
    shape = jax.ShapeDtypeStruct((slots, rows, steps * blocks * columns), BF16)
    keep, give = pl.pallas_call(
        kernel,
        out_shape=[shape, shape],
        grid_spec=pltpu.PrefetchScalarGridSpec(
            num_scalar_prefetch=1,
            grid=(steps,),
            in_specs=in_specs,
            out_specs=[
                pl.BlockSpec((slots, rows, blocks * columns), lambda i, me_ref: (0, 0, i))
            ]
            * 2,
            scratch_shapes=[
                pltpu.VMEM((height, columns) if aligned else (height // rows, rows, columns), F32)
            ],
        ),
        cost_estimate=LIGHT,
        name="weight_grads",
    )(me, *operands)
    return give, keep


class Scatter:
    def __init__(self, cube, give, keep, cut):
        self.cube, self.cut = cube, cut
        self.give, self.keep = [give], [keep]
        self.left = [cube.natural[::-1]]
        self.plan = [[cube.core]] + [list(pair) for pair in zip(cube.near[0][::-1], cube.near[1][::-1])]
        self.plan += [[link] for link in cube.far[::-1]]
        self.step = 0

    def start(self):
        links = self.plan[self.step]
        return [self.cube.swap(give, link) for give, link in zip(self.give, links)]

    def finish(self, got, pieces=None):
        self.step += 1
        rows = self.keep[0].shape[1]
        widths = [k.shape[2] for k in self.keep]
        copies = []
        if self.step == len(self.plan):
            shapes = [
                jax.ShapeDtypeStruct((blocks * rows, wide // blocks), F32)
                for _, wide, blocks in pieces
            ]
            for o, (first, wide, blocks) in enumerate(pieces):
                each = wide // blocks
                for j in range(blocks):
                    low = first + j * each
                    target = (slice(j * rows, (j + 1) * rows), slice(None))
                    copies.append((0, 0, slice(low, low + each), o, target))
            return self.add(got, shapes, copies)
        links = self.plan[self.step]
        if len(links) > len(widths):
            ranges = [(0, 0, self.cut, 0, 0), (0, self.cut, widths[0], 1, 0)]
            self.left = [self.left[0], list(self.left[0])]
            new_widths = [self.cut, widths[0] - self.cut]
        elif len(links) < len(widths):
            ranges = [(0, 0, widths[0], 0, 0), (1, 0, widths[1], 0, widths[0])]
            new_widths = [sum(widths)]
        else:
            ranges = [(i, 0, w, i, 0) for i, w in enumerate(widths)]
            new_widths = widths
        slots = self.keep[0].shape[0]
        for source, low, high, part, first in ranges:
            bit = self.left[part].index(links[part])
            for slot in range(slots):
                side, rest = (slot >> bit) & 1, (slot >> (bit + 1) << bit) | (slot & ((1 << bit) - 1))
                target = (rest, slice(None), slice(first, first + high - low))
                copies.append((source, slot, slice(low, high), 2 * part + side, target))
        shapes = [
            jax.ShapeDtypeStruct((slots // 2, rows, w), BF16) for w in new_widths for _ in range(2)
        ]
        outs = self.add(got, shapes, copies)
        self.keep, self.give = outs[0::2], outs[1::2]
        self.left = [
            [link for link in self.left[i] if link != links[i]] for i in range(len(links))
        ]
        return None

    def add(self, got, shapes, copies):
        count = len(got)
        if self.keep[0].shape[0] <= 2:
            rows = {}
            for source, slot, columns, o, target in copies:
                mine = self.keep[source][slot, :, columns].astype(F32)
                total = (mine + got[source][slot, :, columns].astype(F32)).astype(shapes[o].dtype)
                rows.setdefault(o, []).append(total)
            outs = []
            for o, shape in enumerate(shapes):
                value = rows[o][0] if len(rows[o]) == 1 else jnp.concatenate(rows[o], axis=0)
                outs.append(value.reshape(shape.shape))
            return outs

        def kernel(*refs):
            outs = refs[2 * count :]
            for source, slot, columns, o, target in copies:
                mine = refs[source][slot, :, columns].astype(F32)
                came = refs[count + source][slot, :, columns].astype(F32)
                outs[o][target] = (mine + came).astype(outs[o].dtype)

        total = sum(2 * v.size * 2 for v in self.keep)
        return pl.pallas_call(
            kernel,
            out_shape=shapes,
            in_specs=[pl.BlockSpec(memory_space=pltpu.VMEM)] * (2 * count),
            out_specs=[pl.BlockSpec(memory_space=pltpu.VMEM)] * len(shapes),
            cost_estimate=LIGHT,
            name="add_step",
        )(*self.keep, *got)


def dot_nn(left, right):
    return jnp.dot(left, right, preferred_element_type=F32)


def dot_tn(left, right):
    return lax.dot_general(left, right, (((0,), (0,)), ((), ())), preferred_element_type=F32)


def dot_nt(left, right):
    return lax.dot_general(left, right, (((1,), (1,)), ((), ())), preferred_element_type=F32)


def attend_forward(qkv, query_segment, key_segment):
    rows, width = qkv.shape
    width = width // 3
    blocks = width // LANES

    def kernel(q_ref, k_ref, v_ref, qs_ref, ks_ref, out_ref, lse_ref):
        allowed = ks_ref[...] == qs_ref[...]
        q = q_ref[...] * SCALE
        k = k_ref[...]
        v_t = v_ref[...].T
        lane = lax.broadcasted_iota(jnp.int32, (1, LANES), 1)
        outs = []
        for h in range(LANES // HEAD_DIM):
            k_h = jnp.where(lane // HEAD_DIM == h, k, jnp.zeros_like(k))
            scores = jnp.where(allowed, dot_nt(k_h, q), MASKED)
            top = jnp.max(scores, axis=0, keepdims=True)
            weight = jnp.exp(scores - top)
            total = jnp.sum(weight, axis=0, keepdims=True)
            probs = (weight * (1.0 / total)).astype(BF16)
            outs.append(dot_nn(v_t[h * HEAD_DIM : (h + 1) * HEAD_DIM], probs))
            lse_ref[0, h : h + 1, :] = top + jnp.log(total)
        out_ref[...] = jnp.concatenate(outs, axis=0).T.astype(BF16)

    return pl.pallas_call(
        kernel,
        out_shape=[
            jax.ShapeDtypeStruct((rows, width), BF16),
            jax.ShapeDtypeStruct((blocks, LANES // HEAD_DIM, rows), F32),
        ],
        grid=(blocks,),
        in_specs=[
            pl.BlockSpec((rows, LANES), lambda i: (0, i)),
            pl.BlockSpec((rows, LANES), lambda i: (0, blocks + i)),
            pl.BlockSpec((rows, LANES), lambda i: (0, 2 * blocks + i)),
            pl.BlockSpec((1, rows), lambda i: (0, 0)),
            pl.BlockSpec((rows, 1), lambda i: (0, 0)),
        ],
        out_specs=[
            pl.BlockSpec((rows, LANES), lambda i: (0, i)),
            pl.BlockSpec((1, LANES // HEAD_DIM, rows), lambda i: (i, 0, 0)),
        ],
        cost_estimate=LIGHT,
        name="attend_forward",
    )(qkv, qkv, qkv, query_segment, key_segment)


def attend_backward(qkv, d_attn, lse, query_segment, key_segment):
    rows, width = d_attn.shape
    blocks = width // LANES

    def kernel(q_ref, k_ref, v_ref, d_ref, lse_ref, qs_ref, ks_ref, out_ref):
        allowed = ks_ref[...] == qs_ref[...]
        q = q_ref[...] * SCALE
        k = k_ref[...]
        v = v_ref[...]
        d_out = d_ref[...]
        k_t = k.T
        lane = lax.broadcasted_iota(jnp.int32, (1, LANES), 1)
        d_q, d_k, d_v = [], 0.0, 0.0
        for h in range(LANES // HEAD_DIM):
            here = lane // HEAD_DIM == h
            zero = jnp.zeros_like(k)
            k_h = jnp.where(here, k, zero)
            scores = dot_nt(k_h, q)
            probs = jnp.where(allowed, jnp.exp(scores - lse_ref[0, h : h + 1, :]), 0.0)
            d_out_h = jnp.where(here, d_out, zero)
            d_v = d_v + dot_nn(probs.astype(BF16), d_out_h)
            d_probs = dot_nt(v, d_out_h)
            inner = jnp.sum(probs * d_probs, axis=0, keepdims=True)
            d_scores = (probs * (d_probs - inner)).astype(BF16)
            d_k = d_k + dot_nn(d_scores, jnp.where(here, q, zero))
            d_q.append(dot_nn(k_t[h * HEAD_DIM : (h + 1) * HEAD_DIM], d_scores))
        d_q = jnp.concatenate(d_q, axis=0).T * SCALE
        for part, value in enumerate((d_q, d_k, d_v)):
            place = pl.multiple_of((pl.program_id(0) + part * blocks) * LANES, LANES)
            out_ref[:, pl.ds(place, LANES)] = value.astype(BF16)

    return pl.pallas_call(
        kernel,
        out_shape=jax.ShapeDtypeStruct((rows, 3 * width), BF16),
        grid=(blocks,),
        in_specs=[
            pl.BlockSpec((rows, LANES), lambda i: (0, i)),
            pl.BlockSpec((rows, LANES), lambda i: (0, blocks + i)),
            pl.BlockSpec((rows, LANES), lambda i: (0, 2 * blocks + i)),
            pl.BlockSpec((rows, LANES), lambda i: (0, i)),
            pl.BlockSpec((1, LANES // HEAD_DIM, rows), lambda i: (i, 0, 0)),
            pl.BlockSpec((1, rows), lambda i: (0, 0)),
            pl.BlockSpec((rows, 1), lambda i: (0, 0)),
        ],
        out_specs=pl.BlockSpec((rows, 3 * width), lambda i: (0, 0)),
        cost_estimate=LIGHT,
        name="attend_backward",
    )(qkv, qkv, qkv, d_attn, lse, query_segment, key_segment)


def normalize(stream):
    middle = jnp.mean(stream, axis=-1, keepdims=True)
    centered = stream - middle
    spread = jnp.mean(centered * centered, axis=-1, keepdims=True)
    rho = lax.rsqrt(spread + EPSILON)
    return centered * rho, rho


def normalize_back(grad, gain, hat, rho):
    scaled = grad * gain
    return rho * (
        scaled
        - jnp.mean(scaled, axis=-1, keepdims=True)
        - hat * jnp.mean(scaled * hat, axis=-1, keepdims=True)
    )


def gelu_and_slope(values):
    scale, cubic = math.sqrt(2.0 / math.pi), 0.044715
    square = values * values
    bent = jnp.tanh(scale * (values + cubic * (square * values)))
    half = 0.5 * (1.0 + bent)
    slope = half + 0.5 * values * (1.0 - bent * bent) * (scale * (1.0 + 3.0 * cubic * square))
    return values * half, slope


def layout(lengths, row_count, tile_rows):
    tile_counts = (lengths + tile_rows - 1) // tile_rows
    seg_ends = jnp.cumsum(tile_counts) * tile_rows
    seg_starts = seg_ends - tile_counts * tile_rows
    position = jnp.arange(row_count, dtype=jnp.int32)[:, None]
    inside = (position >= seg_starts[None, :]) & (position < seg_ends[None, :])
    segment = jnp.sum((position >= seg_ends[None, :]).astype(jnp.int32), axis=1)
    offset = jnp.sum(jnp.where(inside, position - seg_starts[None, :], 0), axis=1)
    length_here = jnp.sum(jnp.where(inside, lengths[None, :], 0), axis=1)
    return (segment, offset < length_here)


def col_sums(values):
    return jnp.sum(values.astype(F32), axis=0, keepdims=True)


def per_device(
    tokens,
    cotangent,
    tile_dest,
    seq_lengths,
    norm1_gain,
    norm1_bias,
    w_qkv,
    q_bias,
    v_bias,
    w_out,
    out_bias,
    norm2_gain,
    norm2_bias,
    w_up,
    up_bias,
    w_down,
    down_bias,
):
    dp_size = lax.axis_size("dp")
    peer_count = lax.axis_size("fsdp")
    cube = Cube(dp_size, peer_count)
    my_dp, my_fs = lax.axis_index("dp"), lax.axis_index("fsdp")
    me = jnp.stack([my_dp, my_fs]).astype(jnp.int32)
    tile_count = tile_dest.shape[0]
    row_count, width = tokens.shape
    tile_rows = row_count // tile_count
    shard = w_qkv.shape[0]
    hidden = w_up.shape[1]
    hidden_shard = w_down.shape[0]
    spread = hidden // width

    small = [norm1_gain, norm1_bias, q_bias, v_bias, out_bias, norm2_gain, norm2_bias, down_bias]
    dest_row = jnp.pad(tile_dest.astype(F32), (0, shard - tile_count))
    block = jnp.concatenate(
        [v.reshape(1, shard) for v in small + [dest_row]] + [up_bias.reshape(spread, shard)], axis=0
    )
    block_rows = block.shape[0]
    groups = -(-block_rows // shard)
    block = jnp.pad(block, ((0, groups * shard - block_rows), (0, LANES - shard)))
    if groups > 1:
        block = jnp.concatenate(jnp.split(block, groups, axis=0), axis=1)
    block_width = groups * LANES
    target = tile_dest // tile_count
    tiled = (tile_count, tile_rows, width)
    bucketed = (peer_count, tile_rows, width)

    wide = 3 * width
    half = hidden // 2
    chunk_a = jnp.concatenate([w_qkv, block], axis=1).astype(BF16)
    pieces = [w_out] + [w_up[:, j * width : (j + 1) * width] for j in range(spread)] + [w_down]
    chunk_b = jnp.concatenate([p.astype(BF16) for p in pieces], axis=0)
    full = lax.all_gather(chunk_b, AXES, axis=0, tiled=False)
    mat_out = full[:, :shard].reshape(-1, width)
    mat_up = jnp.concatenate(
        [full[:, (1 + j) * shard : (2 + j) * shard].reshape(-1, width) for j in range(spread)], axis=1
    )
    mat_down = full[:, (1 + spread) * shard :].reshape(hidden, width)
    distance = target ^ my_fs
    token_tiles = after(tokens.reshape(tiled), chunk_a)
    buckets = deal_apart("deal_tokens", distance, token_tiles, peer_count)

    def cross(bucket, d):
        return lax.ppermute(bucket, "fsdp", [(i, i ^ d) for i in range(peer_count)])

    cut_a = (chunk_a.shape[1] // 2 + LANES - 1) // LANES * LANES
    ga = Gather(cube, chunk_a, cut_a)
    steps = len(ga.steps)
    far = sorted(range(peer_count // 2, peer_count), key=lambda d: (d & 1, d))
    near = list(range(1, peer_count // 2))
    groups = [far[k::steps] + near[k::steps] for k in range(steps)]
    got = {0: buckets[0]}
    came_a, landed = [], []
    for k in range(steps):
        came_a.append(ga.advance(*(landed[k - 2] if k >= 2 else [])))
        landed.append([])
        for d in groups[k]:
            got[d] = cross(after(buckets[d], *came_a[k - 1]) if k else buckets[d], d)
            landed[k].append(got[d])
    ga.cores()
    mat_qkv, vectors = ga.matrices(me, [(0, wide, 1), (wide, block_width, 1)])
    devices = dp_size * peer_count
    here = ga.parts[2][:, :, wide - ga.bounds[1] :]
    slots = [cube.masks(slot, cube.far + cube.near[1]) for slot in range(here.shape[0])]
    dest_peers = [mask_f for mask_a, mask_f in slots if mask_a == 0]
    here = jnp.stack([here[i] for i, (mask_a, _) in enumerate(slots) if mask_a == 0])

    def rows_of(blocks, first, count):
        rows = [
            blocks[:, r % shard, (r // shard) * LANES : (r // shard + 1) * LANES]
            for r in range(first, first + count)
        ]
        return jnp.stack(rows, axis=1)

    def spread_lanes(values, size):
        lanes = lax.broadcasted_iota(jnp.int32, (LANES, size), 0)
        places = lax.broadcasted_iota(jnp.int32, (LANES, size), 1)
        return dot_nn(values, (places % shard == lanes).astype(BF16))

    vectors = vectors.reshape(devices, shard, block_width)
    flat = spread_lanes(rows_of(vectors, 0, 8).reshape(devices * 8, LANES), width)
    place = lax.broadcasted_iota(jnp.int32, (devices, 8, width), 2) // shard
    owner = lax.broadcasted_iota(jnp.int32, (devices, 8, width), 0)
    flat = jnp.sum(jnp.where(place == owner, flat.reshape(devices, 8, width), 0.0), axis=0)
    gain_one, shift_one, bias_q, bias_v, bias_out, gain_two, shift_two, bias_down = flat
    count = devices * spread
    flat = spread_lanes(rows_of(vectors, 9, spread).reshape(count, LANES), hidden)
    place = lax.broadcasted_iota(jnp.int32, (count, hidden), 1) // shard
    owner = lax.broadcasted_iota(jnp.int32, (count, hidden), 0)
    bias_up = jnp.sum(jnp.where(place == owner, flat, 0.0), axis=0)

    here = rows_of(here, 8, 1)[:, 0, :tile_count].astype(jnp.int32)
    wanted = my_fs * tile_count + jnp.arange(tile_count, dtype=jnp.int32)
    found = here[None] == wanted[:, None, None]
    dest_peers = jnp.array(dest_peers, dtype=jnp.int32)
    came_far = jnp.sum(jnp.where(found, dest_peers[None, :, None], 0), axis=(1, 2))
    origin = came_far ^ my_fs

    local_tokens = collect(
        "take_tokens", came_far, [got[d] for d in range(peer_count)], tile_count
    ).reshape(row_count, width)
    cot_buckets = deal(
        "deal_cotangent", target, after(cotangent.reshape(tiled), local_tokens), peer_count
    )
    segment, valid_rows = layout(seq_lengths[0], row_count, tile_rows)
    query_segment = segment[None, :]
    key_segment = jnp.where(valid_rows, segment, -1)[:, None]

    stream = local_tokens.astype(F32)
    hat_one, rho_one = normalize(stream)
    norm_one = (hat_one * gain_one + shift_one).astype(BF16)
    qkv_shift = jnp.concatenate([bias_q, jnp.zeros((width,), F32), bias_v])
    norm_one = after(norm_one, cot_buckets)
    qkv_low = (dot_nn(norm_one, mat_qkv) + qkv_shift).astype(BF16)
    got_cot = lax.all_to_all(
        after(cot_buckets, qkv_low), "fsdp", split_axis=0, concat_axis=0, tiled=True
    )
    attn_out, lse = attend_forward(qkv_low, query_segment, key_segment)
    mid_stream = stream + dot_nn(attn_out, mat_out) + bias_out
    hat_two, rho_two = normalize(mid_stream)
    norm_two = (hat_two * gain_two + shift_two).astype(BF16)
    pre_act = dot_nn(norm_two, mat_up) + bias_up
    act_value, gelu_slope = gelu_and_slope(pre_act)
    act_low, gelu_slope = lax.optimization_barrier((act_value.astype(BF16), gelu_slope))
    result = (mid_stream + dot_nn(act_low, mat_down) + bias_down).astype(BF16)
    mixed_buckets = deal("return_mixed", origin, result.reshape(tiled), peer_count)
    got_mixed = lax.all_to_all(mixed_buckets, "fsdp", split_axis=0, concat_axis=0, tiled=True)

    local_cot = deal("take_cotangent", origin, None, after(got_cot, mixed_buckets))
    local_cot = local_cot.reshape(row_count, width)
    grad_out_rows = local_cot.astype(F32) * valid_rows.astype(F32)[:, None]
    grad_out_low = after(grad_out_rows.astype(BF16), mixed_buckets)
    d_down_bias = col_sums(grad_out_low)
    d_w_down = dot_tn(act_low, grad_out_low).astype(BF16)
    sum_down = lax.psum_scatter(d_w_down, AXES, scatter_dimension=0, tiled=True)

    d_act = dot_nt(after(grad_out_low, d_w_down), mat_down)
    d_pre = (d_act * gelu_slope).astype(BF16)

    d_up_bias = col_sums(d_pre)
    d_norm_two = dot_nt(d_pre, mat_up)
    d_gain_two = jnp.sum(d_norm_two * hat_two, axis=0, keepdims=True)
    d_shift_two = jnp.sum(d_norm_two, axis=0, keepdims=True)
    d_mid = grad_out_rows + normalize_back(d_norm_two, gain_two, hat_two, rho_two)
    d_proj_low = d_mid.astype(BF16)
    d_out_bias = col_sums(d_proj_low)
    give, keep = weight_grads(cube, me, [(norm_two, d_pre), (attn_out, d_proj_low)], shard, 1)
    up = Scatter(cube, give, keep, (hidden + width) // 2)
    sent_up = up.start()
    d_attn = dot_nt(after(d_proj_low, give, got_mixed), mat_out).astype(BF16)

    up.finish(tied(sent_up, d_attn))
    sent_up = up.start()
    d_attn = after(d_attn, *up.give)
    d_qkv = attend_backward(qkv_low, d_attn, lse, query_segment, key_segment)
    up.finish(tied(sent_up, d_qkv))
    sent_up = up.start()
    d_qkv = after(d_qkv, *up.give)
    d_q_bias = col_sums(d_qkv[:, :width])
    d_v_bias = col_sums(d_qkv[:, 2 * width :])
    give, keep = weight_grads(cube, me, [(norm_one, d_qkv)], shard, 1)
    qkv = Scatter(cube, give, keep, wide // 2)
    sent_qkv = qkv.start()
    d_norm_one = dot_nt(after(d_qkv, give), mat_qkv)
    d_gain_one = jnp.sum(d_norm_one * hat_one, axis=0, keepdims=True)
    d_shift_one = jnp.sum(d_norm_one, axis=0, keepdims=True)
    d_stream = d_mid + normalize_back(d_norm_one, gain_one, hat_one, rho_one)
    qkv.finish(tied(sent_qkv, d_norm_one))
    sent_qkv = qkv.start()

    tiles = after(d_stream.astype(BF16).reshape(tiled), *qkv.give, *sent_up)
    buckets = deal_apart("return_gradient", came_far, tiles, peer_count)

    d_small = [
        d_gain_one,
        d_shift_one,
        d_q_bias,
        d_v_bias,
        d_out_bias,
        d_gain_two,
        d_shift_two,
        d_down_bias,
    ]
    d_rows = d_small + [d_up_bias[:, j * width : (j + 1) * width] for j in range(spread)]
    value = jnp.concatenate(d_rows, axis=0)
    vector_links = [cube.core] + cube.near[0][::-1] + cube.far[::-1]

    vector_links = [cube.core] + cube.near[0][::-1] + cube.far[::-1]
    up_pieces = [(0, hidden, 1), (hidden, width, 1)]
    got = {0: buckets[0]}
    first = [d for d in far + near if not d & 1]
    second = [d for d in far + near if d & 1]
    waits = [first[:1], first[1:], second[:2], second[2:]]
    for d in first:
        got[d] = cross(buckets[d], d)
    s_qkv = s_up = None
    value = value + cube.swap(value, vector_links[0])
    moved, k = list(buckets), 0
    while s_qkv is None or k + 1 < len(vector_links):
        due = list(moved)
        if k < len(waits):
            due += [got[d] for d in waits[k]]
        if k == 0:
            due.append(sum_down)
        if s_qkv is None:
            came = tied(sent_qkv, *due)
            s_qkv = qkv.finish(came, [(0, wide, 1)])
            if s_qkv is None:
                sent_qkv = qkv.start()
        if k + 1 < len(vector_links):
            value = after(value, *moved)
            value = value + cube.swap(value, vector_links[k + 1])
        moved = came
        if s_up is None:
            s_up = up.finish(tied(sent_up, *moved), up_pieces)
            if s_up is None:
                sent_up = up.start()
        if k == 0:
            for d, bucket in zip(second, tied([buckets[d] for d in second], *moved)):
                got[d] = cross(bucket, d)
        k += 1
    s_rows = value
    grad_tokens = collect(
        "take_gradient", distance, [got[d] for d in range(peer_count)], tile_count
    ).reshape(row_count, width)
    mixed = deal("take_mixed", target, None, after(got_mixed, *buckets)).reshape(row_count, width)
    my_place = my_dp * peer_count + my_fs
    s_block = lax.dynamic_slice(s_rows, (0, my_place * shard), (8, shard))
    s_up_bias = lax.dynamic_slice(
        s_rows[8:].reshape(hidden), (my_place * hidden_shard,), (hidden_shard,)
    )

    return (
        mixed,
        grad_tokens,
        s_block[0],
        s_block[1],
        s_qkv[0],
        s_block[2],
        s_block[3],
        s_up[1],
        s_block[4],
        s_block[5],
        s_block[6],
        s_up[0],
        s_up_bias,
        sum_down.astype(F32),
        s_block[7],
    )


def solution(mesh):
    rows, matrix = P(AXES), P(AXES, None)
    in_specs = (
        matrix,
        matrix,
        rows,
        matrix,
        rows,
        rows,
        matrix,
        rows,
        rows,
        matrix,
        rows,
        rows,
        rows,
        matrix,
        rows,
        matrix,
        rows,
    )
    out_specs = (
        matrix,
        matrix,
        rows,
        rows,
        matrix,
        rows,
        rows,
        matrix,
        rows,
        rows,
        rows,
        matrix,
        rows,
        matrix,
        rows,
    )
    return jax.shard_map(
        per_device, mesh=mesh, in_specs=in_specs, out_specs=out_specs, check_vma=False
    )
```

```python
import math

import jax
import jax.numpy as jnp
from jax import lax
from jax.experimental import pallas as pl
from jax.experimental.pallas import tpu as pltpu
from jax.sharding import PartitionSpec as P

HEAD_DIM = 64
LANES = 128
SCALE = 0.125
EPSILON = 1e-06
MASKED = -1000000000.0
F32 = jnp.float32
BF16 = jnp.bfloat16
AXES = ("dp", "fsdp")
LIGHT = pl.CostEstimate(flops=0, transcendentals=0, bytes_accessed=0)


def bits_of(size):
    return size.bit_length() - 1


class Cube:
    def __init__(self, dp_size, fs_size):
        self.size = {"dp": dp_size, "fsdp": fs_size}
        self.dp_high, self.fs_size = dp_size // 2, fs_size
        high_dp = [("dp", b) for b in reversed(range(1, bits_of(dp_size)))]
        low_fs = [("fsdp", 0)]
        self.core = ("dp", 0)
        self.far = [("fsdp", b) for b in reversed(range(1, bits_of(fs_size)))]
        self.near = (high_dp + low_fs, low_fs + high_dp)
        self.natural = high_dp + self.far + low_fs

    def swap(self, value, link):
        axis, bit = link
        pairs = [(i, i ^ (1 << bit)) for i in range(self.size[axis])]
        return lax.ppermute(value, axis, pairs)

    def masks(self, slot, order):
        found = {"dp": 0, "fsdp": 0}
        for k, (axis, bit) in enumerate(order):
            found[axis] |= ((slot >> k) & 1) << bit
        return found["dp"] >> 1, found["fsdp"]


def move(name, scalars, sources, out_shapes, plan):
    count = len(sources)
    total = sum(2 * s.size * s.dtype.itemsize for s in out_shapes)

    def kernel(scalar_ref, *refs):
        srcs, outs = refs[:count], refs[count : count + len(out_shapes)]
        sems = refs[-1]
        copies = [
            pltpu.make_async_copy(src, out, sems.at[i])
            for i, (src, out) in enumerate(plan(scalar_ref, srcs, outs))
        ]
        for copy in copies:
            copy.start()
        for copy in copies:
            copy.wait()

    class Counter:
        def __getitem__(self, key):
            return jnp.int32(0)

    class Blank:
        @property
        def at(self):
            return self

        def __getitem__(self, key):
            return self

    copies = len(
        plan(Counter(), [Blank() for _ in sources], [Blank() for _ in out_shapes])
    )
    return pl.pallas_call(
        kernel,
        out_shape=out_shapes,
        in_specs=[pl.BlockSpec(memory_space=pltpu.SMEM)]
        + [pl.BlockSpec(memory_space=pl.ANY) for _ in sources],
        out_specs=[pl.BlockSpec(memory_space=pltpu.VMEM) for _ in out_shapes],
        scratch_shapes=[pltpu.SemaphoreType.DMA((copies,))],
        cost_estimate=LIGHT,
        name=name,
    )(scalars, *sources)


def after(value, *others):
    return lax.optimization_barrier((value,) + others)[0]


def tied(values, *others):
    if not others:
        return list(values)
    return list(lax.optimization_barrier(tuple(values) + others)[: len(values)])


class Gather:
    def __init__(self, cube, shard, cut):
        self.cube, self.bounds = cube, (0, cut, shard.shape[1])
        self.parts, self.moved = [shard[None]], []
        self.steps = [[link] for link in cube.far] + [list(pair) for pair in zip(*cube.near)]
        self.step = 0

    def advance(self, *others):
        links, count = self.steps[self.step], len(self.parts)
        parts = tied(self.parts + self.moved, *others)
        parts, moved = parts[:count], parts[count:]
        if moved:
            parts = [jnp.concatenate(pair, axis=0) for pair in zip(parts, moved)]
        if len(links) > len(parts):
            bounds = self.bounds
            parts = [lax.slice_in_dim(parts[0], bounds[i], bounds[i + 1], axis=2) for i in range(2)]
        self.parts = parts
        self.moved = [self.cube.swap(part, link) for part, link in zip(parts, links)]
        self.step += 1
        return self.moved

    def cores(self, *others):
        parts = tied(self.parts + self.moved, *others)
        self.parts = [parts[0], parts[2], parts[1], parts[3]]
        self.others = [self.cube.swap(part, self.cube.core) for part in self.parts]
        return self.others

    def matrices(self, me, pieces, *others):
        cube, bounds = self.cube, self.bounds
        half, rows = self.parts[0].shape[:2]

        def plan(me_ref, srcs, outs):
            core = me_ref[0] & 1
            pairs = []
            for i in range(2):
                order = cube.far + cube.near[i]
                for out, (first, wide, blocks) in zip(outs, pieces):
                    each = wide // blocks
                    for j in range(blocks):
                        low = max(bounds[i], first + j * each)
                        high = min(bounds[i + 1], first + (j + 1) * each)
                        if low >= high:
                            continue
                        taken = pl.ds(low - bounds[i], high - low)
                        placed = pl.ds(low - first - j * each, high - low)
                        for slot in range(2 * half):
                            mask_a, mask_f = cube.masks(slot, order)
                            a, f = (me_ref[0] >> 1) ^ mask_a, me_ref[1] ^ mask_f
                            for k in range(2):
                                src = srcs[4 * k + 2 * i + slot // half].at[slot % half, :, taken]
                                pairs.append((src, out.at[a, core ^ k, f, j, :, placed]))
            return pairs

        shapes = [
            jax.ShapeDtypeStruct(
                (cube.dp_high, 2, cube.fs_size, blocks, rows, wide // blocks), BF16
            )
            for _, wide, blocks in pieces
        ]
        sources = tied(self.parts + self.others, *others)
        outs = move("interleave", me, sources, shapes, plan)
        return [out.reshape(-1, out.shape[-1]) for out in outs]


def deal_apart(name, scalars, tiles, peer_count):
    count, shape = tiles.shape[0], tiles.shape[1:]

    def kernel(far_ref, src, *refs):
        outs, held, sems = refs[:peer_count], refs[-2], refs[-1]
        into = [pltpu.make_async_copy(src.at[i], held.at[i], sems.at[0, i]) for i in range(count)]
        for copy in into:
            copy.start()
        for i in range(count):
            into[i].wait()
            for d in range(peer_count):

                @pl.when(far_ref[i] == d)
                def _():
                    pltpu.make_async_copy(held.at[i], outs[d], sems.at[1, i]).start()

        for i in range(count):
            pltpu.make_async_copy(held.at[i], outs[0], sems.at[1, i]).wait()

    return pl.pallas_call(
        kernel,
        out_shape=[jax.ShapeDtypeStruct(shape, tiles.dtype)] * peer_count,
        in_specs=[pl.BlockSpec(memory_space=pltpu.SMEM), pl.BlockSpec(memory_space=pl.ANY)],
        out_specs=[pl.BlockSpec(memory_space=pl.ANY)] * peer_count,
        scratch_shapes=[
            pltpu.VMEM((count,) + shape, tiles.dtype),
            pltpu.SemaphoreType.DMA((2, count)),
        ],
        cost_estimate=LIGHT,
        name=name,
    )(scalars, tiles)


def collect(name, scalars, buckets, count):
    shape, dtype = buckets[0].shape, buckets[0].dtype
    peer_count = len(buckets)

    def kernel(far_ref, *refs):
        srcs, out, held, sems = refs[:peer_count], refs[peer_count], refs[-2], refs[-1]
        back = [pltpu.make_async_copy(held.at[i], out.at[i], sems.at[1, i]) for i in range(count)]
        for i in range(count):
            for d in range(peer_count):

                @pl.when(far_ref[i] == d)
                def _():
                    pltpu.make_async_copy(srcs[d], held.at[i], sems.at[0, i]).start()

        for i in range(count):
            pltpu.make_async_copy(srcs[0], held.at[i], sems.at[0, i]).wait()
            back[i].start()
        for copy in back:
            copy.wait()

    return pl.pallas_call(
        kernel,
        out_shape=jax.ShapeDtypeStruct((count,) + shape, dtype),
        in_specs=[pl.BlockSpec(memory_space=pltpu.SMEM)]
        + [pl.BlockSpec(memory_space=pl.ANY)] * peer_count,
        out_specs=pl.BlockSpec(memory_space=pl.ANY),
        scratch_shapes=[
            pltpu.VMEM((count,) + shape, dtype),
            pltpu.SemaphoreType.DMA((2, count)),
        ],
        cost_estimate=LIGHT,
        name=name,
    )(scalars, *buckets)


def deal_apart(name, scalars, tiles, peer_count):
    count, shape = tiles.shape[0], tiles.shape[1:]

    def kernel(far_ref, src, *refs):
        outs, held, sems = refs[:peer_count], refs[-2], refs[-1]
        into = [pltpu.make_async_copy(src.at[i], held.at[i], sems.at[0, i]) for i in range(count)]
        for copy in into:
            copy.start()
        for i in range(count):
            into[i].wait()
            for d in range(peer_count):

                @pl.when(far_ref[i] == d)
                def _():
                    pltpu.make_async_copy(held.at[i], outs[d], sems.at[1, i]).start()

        for i in range(count):
            pltpu.make_async_copy(held.at[i], outs[0], sems.at[1, i]).wait()

    return pl.pallas_call(
        kernel,
        out_shape=[jax.ShapeDtypeStruct(shape, tiles.dtype)] * peer_count,
        in_specs=[pl.BlockSpec(memory_space=pltpu.SMEM), pl.BlockSpec(memory_space=pl.ANY)],
        out_specs=[pl.BlockSpec(memory_space=pl.ANY)] * peer_count,
        scratch_shapes=[
            pltpu.VMEM((count,) + shape, tiles.dtype),
            pltpu.SemaphoreType.DMA((2, count)),
        ],
        cost_estimate=LIGHT,
        name=name,
    )(scalars, tiles)


def collect(name, scalars, buckets, count):
    shape, dtype = buckets[0].shape, buckets[0].dtype
    peer_count = len(buckets)

    def kernel(far_ref, *refs):
        srcs, out, held, sems = refs[:peer_count], refs[peer_count], refs[-2], refs[-1]
        back = [pltpu.make_async_copy(held.at[i], out.at[i], sems.at[1, i]) for i in range(count)]
        for i in range(count):
            for d in range(peer_count):

                @pl.when(far_ref[i] == d)
                def _():
                    pltpu.make_async_copy(srcs[d], held.at[i], sems.at[0, i]).start()

        for i in range(count):
            pltpu.make_async_copy(srcs[0], held.at[i], sems.at[0, i]).wait()
            back[i].start()
        for copy in back:
            copy.wait()

    return pl.pallas_call(
        kernel,
        out_shape=jax.ShapeDtypeStruct((count,) + shape, dtype),
        in_specs=[pl.BlockSpec(memory_space=pltpu.SMEM)]
        + [pl.BlockSpec(memory_space=pl.ANY)] * peer_count,
        out_specs=pl.BlockSpec(memory_space=pl.ANY),
        scratch_shapes=[
            pltpu.VMEM((count,) + shape, dtype),
            pltpu.SemaphoreType.DMA((2, count)),
        ],
        cost_estimate=LIGHT,
        name=name,
    )(scalars, *buckets)


def deal(name, peers, tiles, buckets):
    source = buckets if tiles is None else tiles
    count, shape = peers.shape[0], source.shape[1:]
    out_count = count if tiles is None else buckets

    def kernel(peers_ref, src, out, held, sems):
        into, back = [], []
        for i in range(count):
            peer = peers_ref[i]
            here, there = (peer, i) if tiles is None else (i, peer)
            into.append(pltpu.make_async_copy(src.at[here], held.at[i], sems.at[0, i]))
            back.append(pltpu.make_async_copy(held.at[i], out.at[there], sems.at[1, i]))
        for copy in into:
            copy.start()
        for first, second in zip(into, back):
            first.wait()
            second.start()
        for copy in back:
            copy.wait()

    return pl.pallas_call(
        kernel,
        out_shape=jax.ShapeDtypeStruct((out_count,) + shape, source.dtype),
        in_specs=[pl.BlockSpec(memory_space=pltpu.SMEM), pl.BlockSpec(memory_space=pl.ANY)],
        out_specs=pl.BlockSpec(memory_space=pl.ANY),
        scratch_shapes=[
            pltpu.VMEM((count,) + shape, source.dtype),
            pltpu.SemaphoreType.DMA((2, count)),
        ],
        cost_estimate=LIGHT,
        name=name,
    )(peers, source)


def weight_grads(cube, me, jobs, rows, blocks):
    slots = cube.dp_high * cube.fs_size
    order = cube.natural[::-1]
    tokens, height = jobs[0][0].shape
    columns = jobs[0][1].shape[1] if blocks > 1 else min(height, jobs[-1][1].shape[1])
    aligned = rows % 8 == 0
    counts = [right.shape[1] // columns for _, right in jobs]
    starts = [sum(counts[:i]) for i in range(len(jobs))]
    steps = sum(counts)

    def kernel(me_ref, *refs):
        lefts, rights = refs[0 : 2 * len(jobs) : 2], refs[1 : 2 * len(jobs) : 2]
        outs, product = refs[2 * len(jobs) : 2 * len(jobs) + 2], refs[-1]
        step = pl.program_id(0)
        for left, right, start, count in zip(lefts, rights, starts, counts):

            @pl.when((step >= start) & (step < start + count))
            def _():
                value = dot_tn(left[...], right[...])
                if aligned:
                    product[...] = value
                else:
                    for i in range(height // rows):
                        product[i] = value[i * rows : (i + 1) * rows]

        core = me_ref[0] & 1
        for slot in range(slots):
            mask_a, mask_f = cube.masks(slot, order)
            a, f = (me_ref[0] >> 1) ^ mask_a, me_ref[1] ^ mask_f
            for k, out in enumerate(outs):
                owner = (2 * a + (core ^ k)) * cube.fs_size + f
                for j in range(blocks):
                    piece = owner * blocks + j
                    if aligned:
                        value = product[pl.ds(pl.multiple_of(piece * rows, 8), rows), :]
                    else:
                        value = product[piece]
                    out[slot, :, j * columns : (j + 1) * columns] = value.astype(BF16)

    def column(start, count):
        return lambda i, me_ref: (0, jnp.clip(i - start, 0, count - 1))

    in_specs, operands = [], []
    for (left, right), start, count in zip(jobs, starts, counts):
        in_specs.append(pl.BlockSpec((tokens, height), lambda i, me_ref: (0, 0)))
        in_specs.append(pl.BlockSpec((tokens, columns), column(start, count)))
        operands += [left, right]
    shape = jax.ShapeDtypeStruct((slots, rows, steps * blocks * columns), BF16)
    keep, give = pl.pallas_call(
        kernel,
        out_shape=[shape, shape],
        grid_spec=pltpu.PrefetchScalarGridSpec(
            num_scalar_prefetch=1,
            grid=(steps,),
            in_specs=in_specs,
            out_specs=[
                pl.BlockSpec((slots, rows, blocks * columns), lambda i, me_ref: (0, 0, i))
            ]
            * 2,
            scratch_shapes=[
                pltpu.VMEM((height, columns) if aligned else (height // rows, rows, columns), F32)
            ],
        ),
        cost_estimate=LIGHT,
        name="weight_grads",
    )(me, *operands)
    return give, keep


class Scatter:
    def __init__(self, cube, give, keep, cut):
        self.cube, self.cut = cube, cut
        self.give, self.keep = [give], [keep]
        self.left = [cube.natural[::-1]]
        self.plan = [[cube.core]] + [list(pair) for pair in zip(cube.near[0][::-1], cube.near[1][::-1])]
        self.plan += [[link] for link in cube.far[::-1]]
        self.step = 0

    def start(self):
        links = self.plan[self.step]
        return [self.cube.swap(give, link) for give, link in zip(self.give, links)]

    def finish(self, got, pieces=None):
        self.step += 1
        rows = self.keep[0].shape[1]
        widths = [k.shape[2] for k in self.keep]
        copies = []
        if self.step == len(self.plan):
            shapes = [
                jax.ShapeDtypeStruct((blocks * rows, wide // blocks), F32)
                for _, wide, blocks in pieces
            ]
            for o, (first, wide, blocks) in enumerate(pieces):
                each = wide // blocks
                for j in range(blocks):
                    low = first + j * each
                    target = (slice(j * rows, (j + 1) * rows), slice(None))
                    copies.append((0, 0, slice(low, low + each), o, target))
            return self.add(got, shapes, copies)
        links = self.plan[self.step]
        if len(links) > len(widths):
            ranges = [(0, 0, self.cut, 0, 0), (0, self.cut, widths[0], 1, 0)]
            self.left = [self.left[0], list(self.left[0])]
            new_widths = [self.cut, widths[0] - self.cut]
        elif len(links) < len(widths):
            ranges = [(0, 0, widths[0], 0, 0), (1, 0, widths[1], 0, widths[0])]
            new_widths = [sum(widths)]
        else:
            ranges = [(i, 0, w, i, 0) for i, w in enumerate(widths)]
            new_widths = widths
        slots = self.keep[0].shape[0]
        for source, low, high, part, first in ranges:
            bit = self.left[part].index(links[part])
            for slot in range(slots):
                side, rest = (slot >> bit) & 1, (slot >> (bit + 1) << bit) | (slot & ((1 << bit) - 1))
                target = (rest, slice(None), slice(first, first + high - low))
                copies.append((source, slot, slice(low, high), 2 * part + side, target))
        shapes = [
            jax.ShapeDtypeStruct((slots // 2, rows, w), BF16) for w in new_widths for _ in range(2)
        ]
        outs = self.add(got, shapes, copies)
        self.keep, self.give = outs[0::2], outs[1::2]
        self.left = [
            [link for link in self.left[i] if link != links[i]] for i in range(len(links))
        ]
        return None

    def add(self, got, shapes, copies):
        count = len(got)
        if self.keep[0].shape[0] <= 2:
            rows = {}
            for source, slot, columns, o, target in copies:
                mine = self.keep[source][slot, :, columns].astype(F32)
                total = (mine + got[source][slot, :, columns].astype(F32)).astype(shapes[o].dtype)
                rows.setdefault(o, []).append(total)
            outs = []
            for o, shape in enumerate(shapes):
                value = rows[o][0] if len(rows[o]) == 1 else jnp.concatenate(rows[o], axis=0)
                outs.append(value.reshape(shape.shape))
            return outs

        def kernel(*refs):
            outs = refs[2 * count :]
            for source, slot, columns, o, target in copies:
                mine = refs[source][slot, :, columns].astype(F32)
                came = refs[count + source][slot, :, columns].astype(F32)
                outs[o][target] = (mine + came).astype(outs[o].dtype)

        total = sum(2 * v.size * 2 for v in self.keep)
        return pl.pallas_call(
            kernel,
            out_shape=shapes,
            in_specs=[pl.BlockSpec(memory_space=pltpu.VMEM)] * (2 * count),
            out_specs=[pl.BlockSpec(memory_space=pltpu.VMEM)] * len(shapes),
            cost_estimate=LIGHT,
            name="add_step",
        )(*self.keep, *got)


def dot_nn(left, right):
    return jnp.dot(left, right, preferred_element_type=F32)


def dot_tn(left, right):
    return lax.dot_general(left, right, (((0,), (0,)), ((), ())), preferred_element_type=F32)


def dot_nt(left, right):
    return lax.dot_general(left, right, (((1,), (1,)), ((), ())), preferred_element_type=F32)


def attend_forward(qkv, query_segment, key_segment):
    rows, width = qkv.shape
    width = width // 3
    blocks = width // LANES

    def kernel(q_ref, k_ref, v_ref, qs_ref, ks_ref, out_ref, lse_ref):
        allowed = ks_ref[...] == qs_ref[...]
        q = q_ref[...] * SCALE
        k = k_ref[...]
        v_t = v_ref[...].T
        lane = lax.broadcasted_iota(jnp.int32, (1, LANES), 1)
        outs = []
        for h in range(LANES // HEAD_DIM):
            k_h = jnp.where(lane // HEAD_DIM == h, k, jnp.zeros_like(k))
            scores = jnp.where(allowed, dot_nt(k_h, q), MASKED)
            top = jnp.max(scores, axis=0, keepdims=True)
            weight = jnp.exp(scores - top)
            total = jnp.sum(weight, axis=0, keepdims=True)
            probs = (weight * (1.0 / total)).astype(BF16)
            outs.append(dot_nn(v_t[h * HEAD_DIM : (h + 1) * HEAD_DIM], probs))
            lse_ref[0, h : h + 1, :] = top + jnp.log(total)
        out_ref[...] = jnp.concatenate(outs, axis=0).T.astype(BF16)

    return pl.pallas_call(
        kernel,
        out_shape=[
            jax.ShapeDtypeStruct((rows, width), BF16),
            jax.ShapeDtypeStruct((blocks, LANES // HEAD_DIM, rows), F32),
        ],
        grid=(blocks,),
        in_specs=[
            pl.BlockSpec((rows, LANES), lambda i: (0, i)),
            pl.BlockSpec((rows, LANES), lambda i: (0, blocks + i)),
            pl.BlockSpec((rows, LANES), lambda i: (0, 2 * blocks + i)),
            pl.BlockSpec((1, rows), lambda i: (0, 0)),
            pl.BlockSpec((rows, 1), lambda i: (0, 0)),
        ],
        out_specs=[
            pl.BlockSpec((rows, LANES), lambda i: (0, i)),
            pl.BlockSpec((1, LANES // HEAD_DIM, rows), lambda i: (i, 0, 0)),
        ],
        cost_estimate=LIGHT,
        name="attend_forward",
    )(qkv, qkv, qkv, query_segment, key_segment)


def attend_backward(qkv, d_attn, lse, query_segment, key_segment):
    rows, width = d_attn.shape
    blocks = width // LANES

    def kernel(q_ref, k_ref, v_ref, d_ref, lse_ref, qs_ref, ks_ref, out_ref):
        allowed = ks_ref[...] == qs_ref[...]
        q = q_ref[...] * SCALE
        k = k_ref[...]
        v = v_ref[...]
        d_out = d_ref[...]
        k_t = k.T
        lane = lax.broadcasted_iota(jnp.int32, (1, LANES), 1)
        d_q, d_k, d_v = [], 0.0, 0.0
        for h in range(LANES // HEAD_DIM):
            here = lane // HEAD_DIM == h
            zero = jnp.zeros_like(k)
            k_h = jnp.where(here, k, zero)
            scores = dot_nt(k_h, q)
            probs = jnp.where(allowed, jnp.exp(scores - lse_ref[0, h : h + 1, :]), 0.0)
            d_out_h = jnp.where(here, d_out, zero)
            d_v = d_v + dot_nn(probs.astype(BF16), d_out_h)
            d_probs = dot_nt(v, d_out_h)
            inner = jnp.sum(probs * d_probs, axis=0, keepdims=True)
            d_scores = (probs * (d_probs - inner)).astype(BF16)
            d_k = d_k + dot_nn(d_scores, jnp.where(here, q, zero))
            d_q.append(dot_nn(k_t[h * HEAD_DIM : (h + 1) * HEAD_DIM], d_scores))
        d_q = jnp.concatenate(d_q, axis=0).T * SCALE
        for part, value in enumerate((d_q, d_k, d_v)):
            place = pl.multiple_of((pl.program_id(0) + part * blocks) * LANES, LANES)
            out_ref[:, pl.ds(place, LANES)] = value.astype(BF16)

    return pl.pallas_call(
        kernel,
        out_shape=jax.ShapeDtypeStruct((rows, 3 * width), BF16),
        grid=(blocks,),
        in_specs=[
            pl.BlockSpec((rows, LANES), lambda i: (0, i)),
            pl.BlockSpec((rows, LANES), lambda i: (0, blocks + i)),
            pl.BlockSpec((rows, LANES), lambda i: (0, 2 * blocks + i)),
            pl.BlockSpec((rows, LANES), lambda i: (0, i)),
            pl.BlockSpec((1, LANES // HEAD_DIM, rows), lambda i: (i, 0, 0)),
            pl.BlockSpec((1, rows), lambda i: (0, 0)),
            pl.BlockSpec((rows, 1), lambda i: (0, 0)),
        ],
        out_specs=pl.BlockSpec((rows, 3 * width), lambda i: (0, 0)),
        cost_estimate=LIGHT,
        name="attend_backward",
    )(qkv, qkv, qkv, d_attn, lse, query_segment, key_segment)


def normalize(stream):
    middle = jnp.mean(stream, axis=-1, keepdims=True)
    centered = stream - middle
    spread = jnp.mean(centered * centered, axis=-1, keepdims=True)
    rho = lax.rsqrt(spread + EPSILON)
    return centered * rho, rho


def normalize_back(grad, gain, hat, rho):
    scaled = grad * gain
    return rho * (
        scaled
        - jnp.mean(scaled, axis=-1, keepdims=True)
        - hat * jnp.mean(scaled * hat, axis=-1, keepdims=True)
    )


def gelu_and_slope(values):
    scale, cubic = math.sqrt(2.0 / math.pi), 0.044715
    square = values * values
    bent = jnp.tanh(scale * (values + cubic * (square * values)))
    half = 0.5 * (1.0 + bent)
    slope = half + 0.5 * values * (1.0 - bent * bent) * (scale * (1.0 + 3.0 * cubic * square))
    return values * half, slope


def layout(lengths, row_count, tile_rows):
    tile_counts = (lengths + tile_rows - 1) // tile_rows
    seg_ends = jnp.cumsum(tile_counts) * tile_rows
    seg_starts = seg_ends - tile_counts * tile_rows
    position = jnp.arange(row_count, dtype=jnp.int32)[:, None]
    inside = (position >= seg_starts[None, :]) & (position < seg_ends[None, :])
    segment = jnp.sum((position >= seg_ends[None, :]).astype(jnp.int32), axis=1)
    offset = jnp.sum(jnp.where(inside, position - seg_starts[None, :], 0), axis=1)
    length_here = jnp.sum(jnp.where(inside, lengths[None, :], 0), axis=1)
    return (segment, offset < length_here)


def col_sums(values):
    return jnp.sum(values.astype(F32), axis=0, keepdims=True)


def per_device(
    tokens,
    cotangent,
    tile_dest,
    seq_lengths,
    norm1_gain,
    norm1_bias,
    w_qkv,
    q_bias,
    v_bias,
    w_out,
    out_bias,
    norm2_gain,
    norm2_bias,
    w_up,
    up_bias,
    w_down,
    down_bias,
):
    dp_size = lax.axis_size("dp")
    peer_count = lax.axis_size("fsdp")
    cube = Cube(dp_size, peer_count)
    my_dp, my_fs = lax.axis_index("dp"), lax.axis_index("fsdp")
    me = jnp.stack([my_dp, my_fs]).astype(jnp.int32)
    tile_count = tile_dest.shape[0]
    row_count, width = tokens.shape
    tile_rows = row_count // tile_count
    shard = w_qkv.shape[0]
    hidden = w_up.shape[1]
    hidden_shard = w_down.shape[0]
    spread = hidden // width

    small = [norm1_gain, norm1_bias, q_bias, v_bias, out_bias, norm2_gain, norm2_bias, down_bias]
    dest_row = jnp.pad(tile_dest.astype(F32), (0, shard - tile_count))
    block = jnp.concatenate(
        [v.reshape(1, shard) for v in small + [dest_row]] + [up_bias.reshape(spread, shard)], axis=0
    )
    block_rows = block.shape[0]
    groups = -(-block_rows // shard)
    block = jnp.pad(block, ((0, groups * shard - block_rows), (0, LANES - shard)))
    if groups > 1:
        block = jnp.concatenate(jnp.split(block, groups, axis=0), axis=1)
    block_width = groups * LANES
    target = tile_dest // tile_count
    tiled = (tile_count, tile_rows, width)
    bucketed = (peer_count, tile_rows, width)

    wide = 3 * width
    half = hidden // 2
    chunk_a = jnp.concatenate([w_qkv, block], axis=1).astype(BF16)
    pieces = [w_out] + [w_up[:, j * width : (j + 1) * width] for j in range(spread)] + [w_down]
    chunk_b = jnp.concatenate([p.astype(BF16) for p in pieces], axis=0)
    full = lax.all_gather(chunk_b, AXES, axis=0, tiled=False)
    mat_out = full[:, :shard].reshape(-1, width)
    mat_up = jnp.concatenate(
        [full[:, (1 + j) * shard : (2 + j) * shard].reshape(-1, width) for j in range(spread)], axis=1
    )
    mat_down = full[:, (1 + spread) * shard :].reshape(hidden, width)
    distance = target ^ my_fs
    token_tiles = after(tokens.reshape(tiled), chunk_a)
    buckets = deal_apart("deal_tokens", distance, token_tiles, peer_count)

    def cross(bucket, d):
        return lax.ppermute(bucket, "fsdp", [(i, i ^ d) for i in range(peer_count)])

    cut_a = (chunk_a.shape[1] // 2 + LANES - 1) // LANES * LANES
    ga = Gather(cube, chunk_a, cut_a)
    steps = len(ga.steps)
    far = sorted(range(peer_count // 2, peer_count), key=lambda d: (d & 1, d))
    near = list(range(1, peer_count // 2))
    groups = [far[k::steps] + near[k::steps] for k in range(steps)]
    got = {0: buckets[0]}
    came_a, landed = [], []
    for k in range(steps):
        came_a.append(ga.advance(*(landed[k - 2] if k >= 2 else [])))
        landed.append([])
        for d in groups[k]:
            got[d] = cross(after(buckets[d], *came_a[k - 1]) if k else buckets[d], d)
            landed[k].append(got[d])
    ga.cores()
    mat_qkv, vectors = ga.matrices(me, [(0, wide, 1), (wide, block_width, 1)])
    devices = dp_size * peer_count
    here = ga.parts[2][:, :, wide - ga.bounds[1] :]
    slots = [cube.masks(slot, cube.far + cube.near[1]) for slot in range(here.shape[0])]
    dest_peers = [mask_f for mask_a, mask_f in slots if mask_a == 0]
    here = jnp.stack([here[i] for i, (mask_a, _) in enumerate(slots) if mask_a == 0])

    def rows_of(blocks, first, count):
        rows = [
            blocks[:, r % shard, (r // shard) * LANES : (r // shard + 1) * LANES]
            for r in range(first, first + count)
        ]
        return jnp.stack(rows, axis=1)

    def spread_lanes(values, size):
        lanes = lax.broadcasted_iota(jnp.int32, (LANES, size), 0)
        places = lax.broadcasted_iota(jnp.int32, (LANES, size), 1)
        return dot_nn(values, (places % shard == lanes).astype(BF16))

    vectors = vectors.reshape(devices, shard, block_width)
    flat = spread_lanes(rows_of(vectors, 0, 8).reshape(devices * 8, LANES), width)
    place = lax.broadcasted_iota(jnp.int32, (devices, 8, width), 2) // shard
    owner = lax.broadcasted_iota(jnp.int32, (devices, 8, width), 0)
    flat = jnp.sum(jnp.where(place == owner, flat.reshape(devices, 8, width), 0.0), axis=0)
    gain_one, shift_one, bias_q, bias_v, bias_out, gain_two, shift_two, bias_down = flat
    count = devices * spread
    flat = spread_lanes(rows_of(vectors, 9, spread).reshape(count, LANES), hidden)
    place = lax.broadcasted_iota(jnp.int32, (count, hidden), 1) // shard
    owner = lax.broadcasted_iota(jnp.int32, (count, hidden), 0)
    bias_up = jnp.sum(jnp.where(place == owner, flat, 0.0), axis=0)

    here = rows_of(here, 8, 1)[:, 0, :tile_count].astype(jnp.int32)
    wanted = my_fs * tile_count + jnp.arange(tile_count, dtype=jnp.int32)
    found = here[None] == wanted[:, None, None]
    dest_peers = jnp.array(dest_peers, dtype=jnp.int32)
    came_far = jnp.sum(jnp.where(found, dest_peers[None, :, None], 0), axis=(1, 2))
    origin = came_far ^ my_fs

    local_tokens = collect(
        "take_tokens", came_far, [got[d] for d in range(peer_count)], tile_count
    ).reshape(row_count, width)
    cot_buckets = deal(
        "deal_cotangent", target, after(cotangent.reshape(tiled), local_tokens), peer_count
    )
    segment, valid_rows = layout(seq_lengths[0], row_count, tile_rows)
    query_segment = segment[None, :]
    key_segment = jnp.where(valid_rows, segment, -1)[:, None]

    stream = local_tokens.astype(F32)
    hat_one, rho_one = normalize(stream)
    norm_one = (hat_one * gain_one + shift_one).astype(BF16)
    qkv_shift = jnp.concatenate([bias_q, jnp.zeros((width,), F32), bias_v])
    norm_one = after(norm_one, cot_buckets)
    qkv_low = (dot_nn(norm_one, mat_qkv) + qkv_shift).astype(BF16)
    got_cot = lax.all_to_all(
        after(cot_buckets, qkv_low), "fsdp", split_axis=0, concat_axis=0, tiled=True
    )
    attn_out, lse = attend_forward(qkv_low, query_segment, key_segment)
    mid_stream = stream + dot_nn(attn_out, mat_out) + bias_out
    hat_two, rho_two = normalize(mid_stream)
    norm_two = (hat_two * gain_two + shift_two).astype(BF16)
    pre_act = dot_nn(norm_two, mat_up) + bias_up
    act_value, gelu_slope = gelu_and_slope(pre_act)
    act_low, gelu_slope = lax.optimization_barrier((act_value.astype(BF16), gelu_slope))
    result = (mid_stream + dot_nn(act_low, mat_down) + bias_down).astype(BF16)
    mixed_buckets = deal("return_mixed", origin, result.reshape(tiled), peer_count)
    got_mixed = lax.all_to_all(mixed_buckets, "fsdp", split_axis=0, concat_axis=0, tiled=True)

    local_cot = deal("take_cotangent", origin, None, after(got_cot, mixed_buckets))
    local_cot = local_cot.reshape(row_count, width)
    grad_out_rows = local_cot.astype(F32) * valid_rows.astype(F32)[:, None]
    grad_out_low = after(grad_out_rows.astype(BF16), mixed_buckets)
    d_down_bias = col_sums(grad_out_low)
    d_w_down = dot_tn(act_low, grad_out_low).astype(BF16)
    sum_down = lax.psum_scatter(d_w_down, AXES, scatter_dimension=0, tiled=True)

    d_act = dot_nt(after(grad_out_low, d_w_down), mat_down)
    d_pre = (d_act * gelu_slope).astype(BF16)

    d_up_bias = col_sums(d_pre)
    d_norm_two = dot_nt(d_pre, mat_up)
    d_gain_two = jnp.sum(d_norm_two * hat_two, axis=0, keepdims=True)
    d_shift_two = jnp.sum(d_norm_two, axis=0, keepdims=True)
    d_mid = grad_out_rows + normalize_back(d_norm_two, gain_two, hat_two, rho_two)
    d_proj_low = d_mid.astype(BF16)
    d_out_bias = col_sums(d_proj_low)
    give, keep = weight_grads(cube, me, [(norm_two, d_pre), (attn_out, d_proj_low)], shard, 1)
    up = Scatter(cube, give, keep, (hidden + width) // 2)
    sent_up = up.start()
    d_attn = dot_nt(after(d_proj_low, give, got_mixed), mat_out).astype(BF16)

    up.finish(tied(sent_up, d_attn))
    sent_up = up.start()
    d_attn = after(d_attn, *up.give)
    d_qkv = attend_backward(qkv_low, d_attn, lse, query_segment, key_segment)
    up.finish(tied(sent_up, d_qkv))
    sent_up = up.start()
    d_qkv = after(d_qkv, *up.give)
    d_q_bias = col_sums(d_qkv[:, :width])
    d_v_bias = col_sums(d_qkv[:, 2 * width :])
    give, keep = weight_grads(cube, me, [(norm_one, d_qkv)], shard, 1)
    qkv = Scatter(cube, give, keep, wide // 2)
    sent_qkv = qkv.start()
    d_norm_one = dot_nt(after(d_qkv, give), mat_qkv)
    d_gain_one = jnp.sum(d_norm_one * hat_one, axis=0, keepdims=True)
    d_shift_one = jnp.sum(d_norm_one, axis=0, keepdims=True)
    d_stream = d_mid + normalize_back(d_norm_one, gain_one, hat_one, rho_one)
    qkv.finish(tied(sent_qkv, d_norm_one))
    sent_qkv = qkv.start()

    tiles = after(d_stream.astype(BF16).reshape(tiled), *qkv.give, *sent_up)
    buckets = deal_apart("return_gradient", came_far, tiles, peer_count)

    d_small = [
        d_gain_one,
        d_shift_one,
        d_q_bias,
        d_v_bias,
        d_out_bias,
        d_gain_two,
        d_shift_two,
        d_down_bias,
    ]
    d_rows = d_small + [d_up_bias[:, j * width : (j + 1) * width] for j in range(spread)]
    value = jnp.concatenate(d_rows, axis=0)
    vector_links = [cube.core] + cube.near[0][::-1] + cube.far[::-1]

    vector_links = [cube.core] + cube.near[0][::-1] + cube.far[::-1]
    up_pieces = [(0, hidden, 1), (hidden, width, 1)]
    got = {0: buckets[0]}
    first = [d for d in far + near if not d & 1]
    second = [d for d in far + near if d & 1]
    waits = [first, second]
    for d in first:
        got[d] = cross(buckets[d], d)
    for d, bucket in zip(second, tied([buckets[d] for d in second], got[first[0]])):
        got[d] = cross(bucket, d)
    s_qkv = s_up = None
    value = value + cube.swap(value, vector_links[0])
    pending = cube.swap(after(value, *buckets), vector_links[1])
    moved, k = list(buckets), 0
    while s_qkv is None or k + 1 < len(vector_links):
        due = list(moved)
        if k < len(waits):
            due += [got[d] for d in waits[k]]
        if k == 0:
            due.append(sum_down)
        if s_qkv is None:
            came = tied(sent_qkv, *due)
            s_qkv = qkv.finish(came, [(0, wide, 1)])
            if s_qkv is None:
                sent_qkv = qkv.start()
        if pending is not None:
            value = value + after(pending, *(qkv.give if s_qkv is None else came))
            pending = cube.swap(value, vector_links[k + 2]) if k + 2 < len(vector_links) else None
        moved = came
        if s_up is None:
            s_up = up.finish(tied(sent_up, *moved), up_pieces)
            if s_up is None:
                sent_up = up.start()
        k += 1
    s_rows = value
    grad_tokens = collect(
        "take_gradient", distance, [got[d] for d in range(peer_count)], tile_count
    ).reshape(row_count, width)
    mixed = deal("take_mixed", target, None, after(got_mixed, *buckets)).reshape(row_count, width)
    my_place = my_dp * peer_count + my_fs
    s_block = lax.dynamic_slice(s_rows, (0, my_place * shard), (8, shard))
    s_up_bias = lax.dynamic_slice(
        s_rows[8:].reshape(hidden), (my_place * hidden_shard,), (hidden_shard,)
    )

    return (
        mixed,
        grad_tokens,
        s_block[0],
        s_block[1],
        s_qkv[0],
        s_block[2],
        s_block[3],
        s_up[1],
        s_block[4],
        s_block[5],
        s_block[6],
        s_up[0],
        s_up_bias,
        sum_down.astype(F32),
        s_block[7],
    )


def solution(mesh):
    rows, matrix = P(AXES), P(AXES, None)
    in_specs = (
        matrix,
        matrix,
        rows,
        matrix,
        rows,
        rows,
        matrix,
        rows,
        rows,
        matrix,
        rows,
        rows,
        rows,
        matrix,
        rows,
        matrix,
        rows,
    )
    out_specs = (
        matrix,
        matrix,
        rows,
        rows,
        matrix,
        rows,
        rows,
        matrix,
        rows,
        rows,
        rows,
        matrix,
        rows,
        matrix,
        rows,
    )
    return jax.shard_map(
        per_device, mesh=mesh, in_specs=in_specs, out_specs=out_specs, check_vma=False
    )
```
